128 devices in a mesh: wave: 8 (over z, core), row: 16 (over y, x).
Axes of the slice: x: 4, y: 4, z: 4, core: 2. Of those that a mesh axis runs over, the one named last changes fastest.
Arguments:
- lyot_field: bfloat16 [8, 4096, 2, 4096], P('wave', 'row'), may hold values from -6 to 6
- wave_scale: float32 [8], P('wave'), may hold values from 0.35 to 0.7
- trace_start: int32 [8, 1024, 1024], P(None, 'row', 'wave'), may hold values from -8 to 4106, as said below
- trace_length: int32 [8, 1024, 1024], P(None, 'row', 'wave'), may hold values from 1 to 8, as said below
- column_slot: int32 [1024, 1024], P('row', 'wave'), may hold values from 0 to 3
Outputs:
- detector: float32 [4096, 4096], P('row', 'wave')
The draws below stay inside these ranges and needn't reach their ends.
Inputs may be any that keep to these rules, and one draw needn't show every extreme that they name: trace_start[w, v, u] equals 4 v + w plus an offset between -8 and 7; both ends of the offset are reached. `trace_length`: the value 8 is reached.
All inputs are finite; a program needn't handle non-finite values.
Results may differ from the reference program's by a relative error of at most 0.0031.
Values may be sent and summed in bfloat16 or wider, within the bound.
A program may use at most 128 MiB of HBM per device.

```python
import math
import jax
import jax.numpy as jnp
from jax import lax

NP = 4096
NQ = 1024
OFFSET = 8
LMAX = 8
WAVES = 8


def draw_trace_start(key, part):
    offsets = jax.random.randint(key, (WAVES, NQ, NQ), -OFFSET, OFFSET, dtype=jnp.int32)
    offsets = offsets.at[0, 0, 0].set(-OFFSET).at[WAVES - 1, NQ - 1, 0].set(OFFSET - 1)
    wave_pos = jnp.arange(WAVES, dtype=jnp.int32)[:, None, None]
    lens_row = jnp.arange(NQ, dtype=jnp.int32)[None, :, None]
    return 4 * lens_row + wave_pos + offsets


def draw_trace_length(key, part):
    lengths = jax.random.randint(jax.random.fold_in(key, 7), (WAVES, NQ, NQ), 1, LMAX + 1, dtype=jnp.int32)
    return lengths.at[0, 0, 0].set(LMAX)


def set_ends(drawn, key, least, top_value):
    shape = drawn.shape
    place = [jax.random.randint(jax.random.fold_in(key, axis), (), 0, shape[axis]) for axis in range(len(shape))]
    drawn = drawn.at[tuple(place)].set(least)
    longest = shape.index(max(shape))
    place[longest] = (place[longest] + 1) % shape[longest]
    return drawn.at[tuple(place)].set(top_value)


def level_of(key, extent, cuts, smallest, high):
    gain, own = 1.0, jax.random.fold_in(key, 6)
    for axis_at, blocks in cuts:
        heights = jnp.exp(jax.random.uniform(jax.random.fold_in(own, axis_at), (blocks,), jnp.float32, smallest / len(cuts), high / len(cuts)))
        gain = gain * jnp.repeat(heights, extent[axis_at] // blocks).reshape([-1 if axis == axis_at else 1 for axis in range(len(extent))])
    return gain


def noise(rng, extent, deviation, limit, pieces=(), held_as=jnp.bfloat16):
    array = jax.random.normal(rng, extent, jnp.float32) * deviation
    if len(pieces) > 0:
        array = level_of(rng, extent, pieces, -0.22, 0.18) * array
    return jnp.clip(array, min=-limit, max=limit).astype(held_as)


def setup_inputs(seed: int = 0) -> dict:
    arg_keys = jax.random.split(jax.random.key(seed), 6)
    lyot_field = noise(arg_keys[0], (WAVES, NP, 2, NP), 1.0, 6.0, ((0, 8), (1, 16)))
    wave_scale = jnp.clip(jnp.exp(math.log(0.7) - 0.6931472 * jax.random.uniform(arg_keys[1], (WAVES,), jnp.float32) ** level_of(arg_keys[1], (WAVES,), ((0, 8),), -0.2, 0.2)), 0.35, 0.7)
    trace_start = draw_trace_start(jax.random.fold_in(arg_keys[5], 71), 0)
    trace_length = draw_trace_length(jax.random.fold_in(arg_keys[5], 71), 0)
    column_slot = set_ends(jax.random.randint(arg_keys[4], (NQ, NQ), 0, 4), jax.random.fold_in(arg_keys[4], 1), 0, 3).astype(jnp.int32)
    return dict(lyot_field=lyot_field, wave_scale=wave_scale, trace_start=trace_start, trace_length=trace_length, column_slot=column_slot)


def mft_parts(scale):
    pupil_pos = jnp.arange(NP, dtype=jnp.float32) - (NP - 1) / 2.0
    lens_pos = jnp.arange(NQ, dtype=jnp.float32) - (NQ - 1) / 2.0
    phase = pupil_pos[:, None] * lens_pos[None, :] * (scale * (2.0 * math.pi / NP))
    norm = 1.0 / math.sqrt(NP)
    table_real = (jnp.cos(phase) * norm).astype(jnp.bfloat16)
    table_imag = (-jnp.sin(phase) * norm).astype(jnp.bfloat16)
    return (table_real, table_imag)

def intensity_of(pair):
    field, scale = pair
    table_real, table_imag = mft_parts(scale)
    real_part = field[:, 0, :]
    imag_part = field[:, 1, :]
    half_real = jnp.dot(real_part, table_real, preferred_element_type=jnp.float32) - jnp.dot(imag_part, table_imag, preferred_element_type=jnp.float32)
    half_imag = jnp.dot(real_part, table_imag, preferred_element_type=jnp.float32) + jnp.dot(imag_part, table_real, preferred_element_type=jnp.float32)
    half_real = half_real.astype(jnp.bfloat16)
    half_imag = half_imag.astype(jnp.bfloat16)
    lens_real = jnp.dot(half_real.T, table_real, preferred_element_type=jnp.float32) - jnp.dot(half_imag.T, table_imag, preferred_element_type=jnp.float32)
    lens_imag = jnp.dot(half_real.T, table_imag, preferred_element_type=jnp.float32) + jnp.dot(half_imag.T, table_real, preferred_element_type=jnp.float32)
    return lens_real * lens_real + lens_imag * lens_imag

def reference(lyot_field, wave_scale, trace_start, trace_length, column_slot):
    intensity = lax.map(intensity_of, (lyot_field, wave_scale))
    waves_all = lyot_field.shape[0]
    padding = OFFSET + waves_all + LMAX
    detector_cols = 4 * NQ
    total_rows = 4 * NQ + 2 * padding
    deposit = intensity / trace_length.astype(jnp.float32)
    column = 4 * jnp.arange(NQ, dtype=jnp.int32)[None, :] + column_slot
    column = jnp.broadcast_to(column[None, :, :], trace_start.shape)
    top_row = trace_start + padding
    bottom_row = top_row + trace_length
    edges = jnp.zeros((total_rows * detector_cols,), jnp.float32)
    edges = edges.at[(top_row * detector_cols + column).ravel()].add(deposit.ravel())
    edges = edges.at[(bottom_row * detector_cols + column).ravel()].add(-deposit.ravel())
    image = jnp.cumsum(edges.reshape(total_rows, detector_cols), axis=0)
    return image[padding:padding + 4 * NQ]
```

```python
import jax
import jax.numpy as jnp
from jax import lax
from jax.experimental import pallas as pl
from jax.experimental.pallas import tpu as pltpu
from jax.sharding import PartitionSpec as P

F32, BF16, I32 = jnp.float32, jnp.bfloat16, jnp.int32
MESH = pl.DeviceIdType.MESH
NP = 4096
NQ = 1024
ROWS = 16
WAVES = 8
PR = NP // ROWS
QR = NQ // ROWS
UB = NQ // WAVES
EXT = 8
EXTI = 16


def sincos_turns(turns):
    frac = turns - jnp.round(turns)
    quad = jnp.round(frac * 4.0)
    r = (frac - quad * 0.25) * 6.283185307179586
    r2 = r * r
    s = r * (1.0 + r2 * (-1.6666667e-1 + r2 * (8.3333310e-3 + r2 * (-1.9840874e-4 + r2 * 2.7525562e-6))))
    c = 1.0 + r2 * (-0.5 + r2 * (4.16666642e-2 + r2 * (-1.3888397e-3 + r2 * 2.4760495e-5)))
    odd = jnp.abs(quad) == 1.0
    cc = jnp.where(odd, s, c)
    ss = jnp.where(odd, c, s)
    cneg = (quad == 1.0) | (jnp.abs(quad) == 2.0)
    sneg = (quad == -1.0) | (jnp.abs(quad) == 2.0)
    return jnp.where(cneg, -cc, cc), jnp.where(sneg, -ss, ss)


def lens_lanes(shape):
    n = lax.broadcasted_iota(I32, shape, 1)
    i = n % 128
    k = 64 * (n // 128) + i % 64
    return k.astype(F32) - 511.5, i >= 64


def lane_sign(shape):
    return jnp.where(lax.broadcasted_iota(I32, shape, 1) < 64, 1.0, -1.0).astype(F32)


def k1(scale_ref, x_ref, start_ref, length_ref, slot_ref,
       tiles_ref, itop_ref, ibot_ref, stop_ref, sbot_ref, ltop_ref, lbot_ref, ctop_ref, cbot_ref,
       lo_u, lo_v, hi_c, hi_s, tab, acc, sbuf, rbuf, zacc, ibuf,
       y_send, y_recv, i_send, i_recv, e_send, e_recv, t_send, t_recv):
    wave = lax.axis_index("wave")
    row = lax.axis_index("row")
    below = lax.rem(row + 1, ROWS)
    above = lax.rem(row + ROWS - 1, ROWS)

    barrier = pltpu.get_barrier_semaphore()

    def greet_row(i, carry):
        pl.semaphore_signal(barrier, inc=1, device_id=(wave, lax.rem(row + i, ROWS)), device_id_type=MESH)
        return carry

    def greet_wave(i, carry):
        pl.semaphore_signal(barrier, inc=1, device_id=(lax.rem(wave + i, WAVES), row), device_id_type=MESH)
        pl.semaphore_signal(barrier, inc=1, device_id=(lax.rem(wave + i, WAVES), below), device_id_type=MESH)
        pl.semaphore_signal(barrier, inc=1, device_id=(lax.rem(wave + i, WAVES), above), device_id_type=MESH)
        return carry

    lax.fori_loop(1, ROWS, greet_row, 0)
    lax.fori_loop(1, WAVES, greet_wave, 0)

    s = scale_ref[0] * (1.0 / NP)
    y, is_sin = lens_lanes((128, NQ))
    b = lax.broadcasted_iota(I32, (128, NQ), 0).astype(F32) - 63.5
    c, sn = sincos_turns(b * y * s)
    lo_u[...] = jnp.where(is_sin, sn, c) * (1.0 / 64.0)
    lo_v[...] = jnp.where(is_sin, c, -sn) * (1.0 / 64.0)
    y, is_sin = lens_lanes((32, NQ))
    a = lax.broadcasted_iota(I32, (32, NQ), 0).astype(F32) * 128.0 - 1984.0
    c, sn = sincos_turns(a * y * s)
    hi_c[...] = c
    hi_s[...] = sn

    sgn = lane_sign((PR, 128))

    def edge_copies():
        def cp(src, dst, i, dev):
            return pltpu.make_async_remote_copy(src_ref=src, dst_ref=dst, send_sem=t_send.at[i], recv_sem=t_recv.at[i],
                                                device_id=(wave, dev), device_id_type=MESH)
        return [
            cp(start_ref.at[:, QR - EXT:QR, :], stop_ref, 0, below),
            cp(length_ref.at[:, QR - EXT:QR, :], ltop_ref, 1, below),
            cp(slot_ref.at[QR - EXT:QR, :], ctop_ref, 2, below),
            cp(start_ref.at[:, 0:EXT, :], sbot_ref, 3, above),
            cp(length_ref.at[:, 0:EXT, :], lbot_ref, 4, above),
            cp(slot_ref.at[0:EXT, :], cbot_ref, 5, above),
        ]

    def y_copy(dest):
        return pltpu.make_async_remote_copy(src_ref=sbuf.at[dest], dst_ref=rbuf.at[row], send_sem=y_send.at[dest],
                                            recv_sem=y_recv.at[row], device_id=(wave, dest), device_id_type=MESH)

    def y_local():
        return pltpu.make_async_copy(sbuf.at[row], rbuf.at[row], y_recv.at[row])

    def y_arrival(src):
        return pltpu.make_async_remote_copy(src_ref=sbuf.at[src], dst_ref=rbuf.at[src], send_sem=y_send.at[src],
                                            recv_sem=y_recv.at[src], device_id=(wave, src), device_id_type=MESH)

    first = lax.rem(row + row // 4, 4)

    def chunk(t, carry):
        j = lax.rem(first + t, 4)
        lanes = pl.ds(pl.multiple_of(j * 256, 256), 256)

        def make(a, carry):
            rows = pl.ds(pl.multiple_of(a * 128, 128), 128)
            ch = hi_c[pl.ds(a, 1), lanes]
            sh = hi_s[pl.ds(a, 1), lanes]
            tab[j, rows, :] = (lo_u[:, lanes] * ch + lo_v[:, lanes] * sh).astype(BF16)
            return carry

        lax.fori_loop(0, 32, make, 0)
        y = jnp.dot(x_ref[...], tab[j], preferred_element_type=F32)
        acc[0] = y[:, 0:128]
        acc[1] = y[:, 128:256]

        @pl.when(t == 0)
        def _():
            pl.semaphore_wait(barrier, 36)
            for copy in edge_copies():
                copy.start()

        for half in range(2):
            p = acc[half, pl.ds(0, PR, stride=2), :]
            r = pltpu.roll(acc[half, pl.ds(1, PR, stride=2), :], 64, 1)
            direct = 2 * j + half
            mirror = ROWS - 1 - direct
            sbuf[direct] = (r + sgn * p).astype(BF16)
            sbuf[mirror] = (p - sgn * r).astype(BF16)
            for dest in (direct, mirror):
                @pl.when(dest != row)
                def _():
                    y_copy(dest).start()

                @pl.when(dest == row)
                def _():
                    y_local().start()
        return carry

    lax.fori_loop(0, 4, chunk, 0)

    zacc[...] = jnp.zeros_like(zacc)

    def absorb(t, carry):
        src = lax.rem(row + t, ROWS)

        @pl.when(t == 0)
        def _():
            y_local().wait()

        @pl.when(t != 0)
        def _():
            y_arrival(src).wait_recv()

        rows = pl.ds(pl.multiple_of(src * PR, PR), PR)
        m = rbuf[src]
        for j in range(4):
            zacc[:, 256 * j:256 * j + 256] += lax.dot_general(
                m, tab[j, rows, :], (((0,), (0,)), ((), ())), preferred_element_type=F32)
        return carry

    lax.fori_loop(0, ROWS, absorb, 0)

    sgz = lane_sign((QR, 128))
    low = lax.broadcasted_iota(I32, (QR, 128), 1) < 64
    rev = (lax.broadcasted_iota(I32, (UB, UB), 0) + lax.broadcasted_iota(I32, (UB, UB), 1) == UB - 1).astype(BF16)
    ri = lax.broadcasted_iota(I32, (QR, QR), 0)
    ci = lax.broadcasted_iota(I32, (QR, QR), 1)
    order = jnp.where(row >= ROWS // 2, (ri + ci == QR - 1).astype(F32), (ri == ci).astype(F32)).astype(BF16)
    for m in range(4):
        direct, mirror = [], []
        for blk in (2 * m, 2 * m + 1):
            cols = slice(128 * blk, 128 * blk + 128)
            p = zacc[0:QR, cols]
            r = pltpu.roll(zacc[QR:2 * QR, cols], 64, 1)
            z1 = r + sgz * p
            z2 = p - sgz * r
            z1 = z1 * z1
            z2 = z2 * z2
            direct.append(z1 + pltpu.roll(z1, 64, 1))
            mirror.append(z2 + pltpu.roll(z2, 64, 1))
        d = jnp.where(low, direct[0], direct[1]).astype(BF16)
        q = jnp.where(low, mirror[0], mirror[1]).astype(BF16)
        q = jnp.dot(q, rev, preferred_element_type=F32).astype(BF16)
        ibuf[m] = jnp.dot(order, d, preferred_element_type=F32).astype(BF16)
        ibuf[WAVES - 1 - m] = jnp.dot(order, q, preferred_element_type=F32).astype(BF16)

    def i_copy(dest):
        return pltpu.make_async_remote_copy(src_ref=ibuf.at[dest], dst_ref=tiles_ref.at[wave], send_sem=i_send.at[dest],
                                            recv_sem=i_recv.at[wave], device_id=(dest, row), device_id_type=MESH)

    def top_copy(dest):
        return pltpu.make_async_remote_copy(src_ref=ibuf.at[dest, QR - EXTI:QR, :], dst_ref=itop_ref.at[wave], send_sem=e_send.at[0, dest],
                                            recv_sem=e_recv.at[0, wave], device_id=(dest, below), device_id_type=MESH)

    def bot_copy(dest):
        return pltpu.make_async_remote_copy(src_ref=ibuf.at[dest, 0:EXTI, :], dst_ref=ibot_ref.at[wave], send_sem=e_send.at[1, dest],
                                            recv_sem=e_recv.at[1, wave], device_id=(dest, above), device_id_type=MESH)

    def own():
        return pltpu.make_async_copy(ibuf.at[wave], tiles_ref.at[wave], i_recv.at[wave])

    def send(t, carry):
        dest = lax.rem(wave + t, WAVES)
        top_copy(dest).start()
        bot_copy(dest).start()

        @pl.when(t != 0)
        def _():
            i_copy(dest).start()

        @pl.when(t == 0)
        def _():
            own().start()
        return carry

    lax.fori_loop(0, WAVES, send, 0)

    def i_arrival(src):
        return pltpu.make_async_remote_copy(src_ref=ibuf.at[src], dst_ref=tiles_ref.at[src], send_sem=i_send.at[src],
                                            recv_sem=i_recv.at[src], device_id=(src, row), device_id_type=MESH)

    def top_arrival(src):
        return pltpu.make_async_remote_copy(src_ref=ibuf.at[src, QR - EXTI:QR, :], dst_ref=itop_ref.at[src], send_sem=e_send.at[0, src],
                                            recv_sem=e_recv.at[0, src], device_id=(src, below), device_id_type=MESH)

    def bot_arrival(src):
        return pltpu.make_async_remote_copy(src_ref=ibuf.at[src, 0:EXTI, :], dst_ref=ibot_ref.at[src], send_sem=e_send.at[1, src],
                                            recv_sem=e_recv.at[1, src], device_id=(src, above), device_id_type=MESH)

    def finish(t, carry):
        src = lax.rem(wave + t, WAVES)

        @pl.when(t != 0)
        def _():
            i_arrival(src).wait()

        @pl.when(t == 0)
        def _():
            own().wait()
        top_arrival(src).wait()
        bot_arrival(src).wait()
        return carry

    lax.fori_loop(0, WAVES, finish, 0)

    def drain(t, carry):
        y_copy(lax.rem(row + t, ROWS)).wait_send()
        return carry

    lax.fori_loop(1, ROWS, drain, 0)
    for copy in edge_copies():
        copy.wait()


PAIRS = 36
ACC_ROWS = 8 * PAIRS + 40


def k2(tiles_ref, itop_ref, ibot_ref, start_ref, stop_ref, sbot_ref, length_ref, ltop_ref, lbot_ref,
       slot_ref, ctop_ref, cbot_ref, out_ref, f_s, e_s, a_s, c_s, acc):
    row = lax.axis_index("row")
    first_lens = row * QR

    def put(at, count, light, start, length, slot):
        base = 4 * (first_lens + at - EXT + lax.broadcasted_iota(I32, (1, count, UB), 1)) - 8
        base = base - 4 * (lax.broadcasted_iota(I32, (1, count, UB), 1) % 2)
        begin = start - base
        f_s[:, at:at + count, :] = begin
        e_s[:, at:at + count, :] = begin + length
        a_s[:, at:at + count, :] = light / length.astype(F32)
        c_s[at:at + count, :] = slot

    top = EXTI - EXT
    put(0, EXT, itop_ref[...].astype(F32)[:, top:, :], stop_ref[...], ltop_ref[...], ctop_ref[...])
    put(EXT, QR, tiles_ref[...].astype(F32), start_ref[...], length_ref[...], slot_ref[...])
    put(EXT + QR, EXT, ibot_ref[...].astype(F32)[:, :EXT, :], sbot_ref[...], lbot_ref[...], cbot_ref[...])
    acc[...] = jnp.zeros_like(acc)
    sub = lax.broadcasted_iota(I32, (8, UB), 0)

    def pair(j, carry):
        light = [[jnp.zeros((8, UB), F32) for _ in range(5)] for _ in range(4)]
        for odd in range(2):
            q = 2 * (j + 1) + odd
            strip = [None] * 5
            for w in range(WAVES):
                f = jnp.broadcast_to(f_s[w, pl.ds(q, 1), :], (8, UB))
                e = jnp.broadcast_to(e_s[w, pl.ds(q, 1), :], (8, UB))
                v = jnp.broadcast_to(a_s[w, pl.ds(q, 1), :], (8, UB))
                least, most = w + 4 * odd, w + 4 * odd + 22
                for i in range(least // 8, most // 8 + 1):
                    h = sub + 8 * i
                    add = jnp.where((h >= f) & (h < e), v, 0.0)
                    strip[i] = add if strip[i] is None else strip[i] + add
            c = jnp.broadcast_to(c_s[pl.ds(q, 1), :], (8, UB))
            for k in range(4):
                hot = c == k
                for i in range(5):
                    if strip[i] is not None:
                        light[k][i] = light[k][i] + jnp.where(hot, strip[i], 0.0)
        for k in range(4):
            for i in range(5):
                rows = pl.ds(pl.multiple_of(8 * j + 8 * i, 8), 8)
                acc[rows, UB * k:UB * k + UB] += light[k][i]
        return carry

    lax.fori_loop(0, PAIRS, pair, 0)
    image = acc[32:32 + 4 * QR, :]
    hi = image.astype(BF16)
    lo = (image - hi.astype(F32)).astype(BF16)
    n = lax.broadcasted_iota(I32, (4 * UB, 4 * UB), 0)
    x = lax.broadcasted_iota(I32, (4 * UB, 4 * UB), 1)
    spread = (4 * (n % UB) + n // UB == x).astype(F32).astype(BF16)
    out_ref[...] = jnp.dot(hi, spread, preferred_element_type=F32) + jnp.dot(lo, spread, preferred_element_type=F32)


def per_device(lyot_field, wave_scale, trace_start, trace_length, column_slot):
    x = lyot_field.reshape(2 * PR, NP)
    vm = pl.BlockSpec(memory_space=pltpu.VMEM)
    hbm = pl.BlockSpec(memory_space=pl.ANY)
    sds = jax.ShapeDtypeStruct
    dma = pltpu.SemaphoreType.DMA
    tiles, itop, ibot, stop, sbot, ltop, lbot, ctop, cbot = pl.pallas_call(
        k1,
        out_shape=[
            sds((WAVES, QR, UB), BF16), sds((WAVES, EXTI, UB), BF16), sds((WAVES, EXTI, UB), BF16),
            sds((WAVES, EXT, UB), I32), sds((WAVES, EXT, UB), I32), sds((WAVES, EXT, UB), I32), sds((WAVES, EXT, UB), I32),
            sds((EXT, UB), I32), sds((EXT, UB), I32),
        ],
        in_specs=[pl.BlockSpec(memory_space=pltpu.SMEM), vm, vm, vm, vm],
        out_specs=[vm] * 9,
        scratch_shapes=[
            pltpu.VMEM((128, NQ), F32), pltpu.VMEM((128, NQ), F32), pltpu.VMEM((32, NQ), F32), pltpu.VMEM((32, NQ), F32),
            pltpu.VMEM((4, NP, 256), BF16), pltpu.VMEM((2, 2 * PR, 128), F32),
            pltpu.VMEM((ROWS, PR, 128), BF16), pltpu.VMEM((ROWS, PR, 128), BF16),
            pltpu.VMEM((2 * QR, NQ), F32), pltpu.VMEM((WAVES, QR, UB), BF16),
            dma((ROWS,)), dma((ROWS,)), dma((WAVES,)), dma((WAVES,)), dma((2, WAVES)), dma((2, WAVES)), dma((6,)), dma((6,)),
        ],
        compiler_params=pltpu.CompilerParams(collective_id=0, has_side_effects=True, vmem_limit_bytes=48 << 20),
    )(wave_scale, x, trace_start, trace_length, column_slot)
    return pl.pallas_call(
        k2,
        out_shape=sds((4 * QR, 4 * UB), F32),
        in_specs=[vm] * 12,
        out_specs=vm,
        scratch_shapes=[
            pltpu.VMEM((WAVES, QR + 2 * EXT, UB), I32), pltpu.VMEM((WAVES, QR + 2 * EXT, UB), I32),
            pltpu.VMEM((WAVES, QR + 2 * EXT, UB), F32), pltpu.VMEM((QR + 2 * EXT, UB), I32),
            pltpu.VMEM((ACC_ROWS, 4 * UB), F32),
        ],
    )(tiles, itop, ibot, trace_start, stop, sbot, trace_length, ltop, lbot, column_slot, ctop, cbot)


def solution(mesh):
    placed = (
        P("wave", "row", None, None),
        P("wave"),
        P(None, "row", "wave"),
        P(None, "row", "wave"),
        P("row", "wave"),
    )
    return jax.shard_map(
        per_device, mesh=mesh, in_specs=placed, out_specs=P("row", "wave"), check_vma=False
    )
```

```python
import jax
import jax.numpy as jnp
from jax import lax
from jax.experimental import pallas as pl
from jax.experimental.pallas import tpu as pltpu
from jax.sharding import PartitionSpec as P

F32, BF16, I32 = jnp.float32, jnp.bfloat16, jnp.int32
MESH = pl.DeviceIdType.MESH
NP = 4096
NQ = 1024
ROWS = 16
WAVES = 8
PR = NP // ROWS
QR = NQ // ROWS
UB = NQ // WAVES
EXT = 8
EXTI = 16


def sincos_turns(turns):
    frac = turns - jnp.round(turns)
    quad = jnp.round(frac * 4.0)
    r = (frac - quad * 0.25) * 6.283185307179586
    r2 = r * r
    s = r * (1.0 + r2 * (-1.6666667e-1 + r2 * (8.3333310e-3 + r2 * (-1.9840874e-4 + r2 * 2.7525562e-6))))
    c = 1.0 + r2 * (-0.5 + r2 * (4.16666642e-2 + r2 * (-1.3888397e-3 + r2 * 2.4760495e-5)))
    odd = jnp.abs(quad) == 1.0
    cc = jnp.where(odd, s, c)
    ss = jnp.where(odd, c, s)
    cneg = (quad == 1.0) | (jnp.abs(quad) == 2.0)
    sneg = (quad == -1.0) | (jnp.abs(quad) == 2.0)
    return jnp.where(cneg, -cc, cc), jnp.where(sneg, -ss, ss)


def lens_lanes(shape, first):
    n = lax.broadcasted_iota(I32, shape, 1) + first
    i = n % 128
    k = 64 * (n // 128) + i % 64
    return k.astype(F32) - 511.5, i >= 64


def lane_sign(shape):
    return jnp.where(lax.broadcasted_iota(I32, shape, 1) < 64, 1.0, -1.0).astype(F32)


def k1(scale_ref, x_ref, start_ref, length_ref, slot_ref,
       tiles_ref, itop_ref, ibot_ref, stop_ref, sbot_ref, ltop_ref, lbot_ref, ctop_ref, cbot_ref,
       xv, lo_u, lo_v, hi_c, hi_s, tab, acc, sbuf, rbuf, zacc, ibuf,
       y_send, y_recv, i_send, i_recv, e_send, e_recv, t_send, t_recv, x_sem):
    wave = lax.axis_index("wave")
    row = lax.axis_index("row")
    below = lax.rem(row + 1, ROWS)
    above = lax.rem(row + ROWS - 1, ROWS)

    def fetch(c):
        return pltpu.make_async_copy(x_ref.at[:, c], xv.at[c], x_sem.at[c])

    for c in range(32):
        fetch(c).start()

    barrier = pltpu.get_barrier_semaphore()

    def greet_row(i, carry):
        pl.semaphore_signal(barrier, inc=1, device_id=(wave, lax.rem(row + i, ROWS)), device_id_type=MESH)
        return carry

    def greet_wave(i, carry):
        pl.semaphore_signal(barrier, inc=1, device_id=(lax.rem(wave + i, WAVES), row), device_id_type=MESH)
        pl.semaphore_signal(barrier, inc=1, device_id=(lax.rem(wave + i, WAVES), below), device_id_type=MESH)
        pl.semaphore_signal(barrier, inc=1, device_id=(lax.rem(wave + i, WAVES), above), device_id_type=MESH)
        return carry

    lax.fori_loop(1, ROWS, greet_row, 0)
    lax.fori_loop(1, WAVES, greet_wave, 0)

    s = scale_ref[0] * (1.0 / NP)
    for j in range(2):
        y, is_sin = lens_lanes((128, 512), 512 * j)
        b = lax.broadcasted_iota(I32, (128, 512), 0).astype(F32) - 63.5
        c, sn = sincos_turns(b * y * s)
        lo_u[j] = jnp.where(is_sin, sn, c) * (1.0 / 64.0)
        lo_v[j] = jnp.where(is_sin, c, -sn) * (1.0 / 64.0)
        y, is_sin = lens_lanes((32, 512), 512 * j)
        a = lax.broadcasted_iota(I32, (32, 512), 0).astype(F32) * 128.0 - 1984.0
        c, sn = sincos_turns(a * y * s)
        hi_c[j] = c
        hi_s[j] = sn

    def make(i, carry):
        j = i // 32
        a = lax.rem(i, 32)
        rows = pl.ds(pl.multiple_of(a * 128, 128), 128)
        ch = hi_c[j, pl.ds(a, 1), :]
        sh = hi_s[j, pl.ds(a, 1), :]
        tab[j, rows, :] = (lo_u[j] * ch + lo_v[j] * sh).astype(BF16)
        return carry

    lax.fori_loop(0, 64, make, 0)

    sgn = lane_sign((PR, 128))

    def edge_copies():
        def cp(src, dst, i, dev):
            return pltpu.make_async_remote_copy(src_ref=src, dst_ref=dst, send_sem=t_send.at[i], recv_sem=t_recv.at[i],
                                                device_id=(wave, dev), device_id_type=MESH)
        return [
            cp(start_ref.at[:, QR - EXT:QR, :], stop_ref, 0, below),
            cp(length_ref.at[:, QR - EXT:QR, :], ltop_ref, 1, below),
            cp(slot_ref.at[QR - EXT:QR, :], ctop_ref, 2, below),
            cp(start_ref.at[:, 0:EXT, :], sbot_ref, 3, above),
            cp(length_ref.at[:, 0:EXT, :], lbot_ref, 4, above),
            cp(slot_ref.at[0:EXT, :], cbot_ref, 5, above),
        ]

    def y_copy(dest):
        return pltpu.make_async_remote_copy(src_ref=sbuf.at[dest], dst_ref=rbuf.at[row], send_sem=y_send.at[dest],
                                            recv_sem=y_recv.at[row], device_id=(wave, dest), device_id_type=MESH)

    def y_local():
        return pltpu.make_async_copy(sbuf.at[row], rbuf.at[row], y_recv.at[row])

    def y_arrival(src):
        return pltpu.make_async_remote_copy(src_ref=sbuf.at[src], dst_ref=rbuf.at[src], send_sem=y_send.at[src],
                                            recv_sem=y_recv.at[src], device_id=(wave, src), device_id_type=MESH)

    def field(g, count):
        return jnp.concatenate([xv.at[g + c].reshape(2 * PR, 128)[...] for c in range(count)], axis=1)

    first = lax.rem(row, 2)
    for t in range(2):
        j = first if t == 0 else 1 - first
        if t == 0:
            for g in range(4):
                for c in range(8 * g, 8 * g + 8):
                    fetch(c).wait()
                y = jnp.dot(field(8 * g, 8), tab[j, 1024 * g:1024 * g + 1024, :], preferred_element_type=F32)
                for i in range(4):
                    if g == 0:
                        acc[i] = y[:, 128 * i:128 * i + 128]
                    else:
                        acc[i] += y[:, 128 * i:128 * i + 128]
            pl.semaphore_wait(barrier, 36)
        else:
            y = jnp.dot(field(0, 32), tab[j], preferred_element_type=F32)
            for i in range(4):
                acc[i] = y[:, 128 * i:128 * i + 128]

        def message(i, carry):
            p = acc[i, pl.ds(0, PR, stride=2), :]
            r = pltpu.roll(acc[i, pl.ds(1, PR, stride=2), :], 64, 1)
            direct = 4 * j + i
            mirror = ROWS - 1 - direct
            sbuf[direct] = (r + sgn * p).astype(BF16)
            sbuf[mirror] = (p - sgn * r).astype(BF16)
            for dest in (direct, mirror):
                @pl.when(dest != row)
                def _():
                    y_copy(dest).start()

                @pl.when(dest == row)
                def _():
                    y_local().start()
            return carry

        lax.fori_loop(0, 4, message, 0)
        if t == 0:
            for copy in edge_copies():
                copy.start()

    zacc[...] = jnp.zeros_like(zacc)
    half = row // 4
    early = jnp.where((half == 0) | (half == 3), 0, 1)

    def source(i):
        return 2 * lax.rem(row // 2 + i, 8) + jnp.where(i < 8, early, 1 - early)

    def absorb(t, carry):
        srcs = [source(4 * t + i) for i in range(4)]
        for src in srcs:
            @pl.when(src == row)
            def _():
                y_local().wait()

            @pl.when(src != row)
            def _():
                y_arrival(src).wait_recv()

        for j in range(2):
            total = None
            for src in srcs:
                rows = pl.ds(pl.multiple_of(src * PR, PR), PR)
                z = lax.dot_general(rbuf[src], tab[j, rows, :], (((0,), (0,)), ((), ())), preferred_element_type=F32)
                total = z if total is None else total + z
            zacc[:, 512 * j:512 * j + 512] += total
        return carry

    lax.fori_loop(0, 4, absorb, 0)

    sgz = lane_sign((QR, 128))
    low = lax.broadcasted_iota(I32, (QR, 128), 1) < 64
    rev = (lax.broadcasted_iota(I32, (UB, UB), 0) + lax.broadcasted_iota(I32, (UB, UB), 1) == UB - 1).astype(BF16)
    ri = lax.broadcasted_iota(I32, (QR, QR), 0)
    ci = lax.broadcasted_iota(I32, (QR, QR), 1)
    order = jnp.where(row >= ROWS // 2, (ri + ci == QR - 1).astype(F32), (ri == ci).astype(F32)).astype(BF16)
    def i_copy(dest):
        return pltpu.make_async_remote_copy(src_ref=ibuf.at[dest], dst_ref=tiles_ref.at[wave], send_sem=i_send.at[dest],
                                            recv_sem=i_recv.at[wave], device_id=(dest, row), device_id_type=MESH)

    def top_copy(dest):
        return pltpu.make_async_remote_copy(src_ref=ibuf.at[dest, QR - EXTI:QR, :], dst_ref=itop_ref.at[wave], send_sem=e_send.at[0, dest],
                                            recv_sem=e_recv.at[0, wave], device_id=(dest, below), device_id_type=MESH)

    def bot_copy(dest):
        return pltpu.make_async_remote_copy(src_ref=ibuf.at[dest, 0:EXTI, :], dst_ref=ibot_ref.at[wave], send_sem=e_send.at[1, dest],
                                            recv_sem=e_recv.at[1, wave], device_id=(dest, above), device_id_type=MESH)

    def own():
        return pltpu.make_async_copy(ibuf.at[wave], tiles_ref.at[wave], i_recv.at[wave])

    for m in range(4):
        direct, mirror = [], []
        for blk in (2 * m, 2 * m + 1):
            cols = slice(128 * blk, 128 * blk + 128)
            p = zacc[0:QR, cols]
            r = pltpu.roll(zacc[QR:2 * QR, cols], 64, 1)
            z1 = r + sgz * p
            z2 = p - sgz * r
            z1 = z1 * z1
            z2 = z2 * z2
            direct.append(z1 + pltpu.roll(z1, 64, 1))
            mirror.append(z2 + pltpu.roll(z2, 64, 1))
        d = jnp.where(low, direct[0], direct[1]).astype(BF16)
        q = jnp.where(low, mirror[0], mirror[1]).astype(BF16)
        q = jnp.dot(q, rev, preferred_element_type=F32).astype(BF16)
        ibuf[m] = jnp.dot(order, d, preferred_element_type=F32).astype(BF16)
        ibuf[WAVES - 1 - m] = jnp.dot(order, q, preferred_element_type=F32).astype(BF16)
        for dest in (m, WAVES - 1 - m):
            top_copy(dest).start()
            bot_copy(dest).start()

            @pl.when(dest != wave)
            def _():
                i_copy(dest).start()

            @pl.when(dest == wave)
            def _():
                own().start()

    def i_arrival(src):
        return pltpu.make_async_remote_copy(src_ref=ibuf.at[src], dst_ref=tiles_ref.at[src], send_sem=i_send.at[src],
                                            recv_sem=i_recv.at[src], device_id=(src, row), device_id_type=MESH)

    def top_arrival(src):
        return pltpu.make_async_remote_copy(src_ref=ibuf.at[src, QR - EXTI:QR, :], dst_ref=itop_ref.at[src], send_sem=e_send.at[0, src],
                                            recv_sem=e_recv.at[0, src], device_id=(src, below), device_id_type=MESH)

    def bot_arrival(src):
        return pltpu.make_async_remote_copy(src_ref=ibuf.at[src, 0:EXTI, :], dst_ref=ibot_ref.at[src], send_sem=e_send.at[1, src],
                                            recv_sem=e_recv.at[1, src], device_id=(src, above), device_id_type=MESH)

    def finish(t, carry):
        src = lax.rem(wave + t, WAVES)

        @pl.when(t != 0)
        def _():
            i_arrival(src).wait()

        @pl.when(t == 0)
        def _():
            own().wait()
        top_arrival(src).wait()
        bot_arrival(src).wait()
        return carry

    lax.fori_loop(0, WAVES, finish, 0)

    def drain(t, carry):
        y_copy(lax.rem(row + t, ROWS)).wait_send()
        return carry

    lax.fori_loop(1, ROWS, drain, 0)
    for copy in edge_copies():
        copy.wait()


PAIRS = 36
ACC_ROWS = 8 * PAIRS + 40


def k2(tiles_ref, itop_ref, ibot_ref, start_ref, stop_ref, sbot_ref, length_ref, ltop_ref, lbot_ref,
       slot_ref, ctop_ref, cbot_ref, out_ref, f_s, e_s, a_s, c_s, acc):
    row = lax.axis_index("row")
    first_lens = row * QR

    def put(at, count, light, start, length, slot):
        base = 4 * (first_lens + at - EXT + lax.broadcasted_iota(I32, (1, count, UB), 1)) - 8
        base = base - 4 * (lax.broadcasted_iota(I32, (1, count, UB), 1) % 2)
        begin = start - base
        f_s[:, at:at + count, :] = begin
        e_s[:, at:at + count, :] = begin + length
        a_s[:, at:at + count, :] = light / length.astype(F32)
        c_s[at:at + count, :] = slot

    top = EXTI - EXT
    put(0, EXT, itop_ref[...].astype(F32)[:, top:, :], stop_ref[...], ltop_ref[...], ctop_ref[...])
    put(EXT, QR, tiles_ref[...].astype(F32), start_ref[...], length_ref[...], slot_ref[...])
    put(EXT + QR, EXT, ibot_ref[...].astype(F32)[:, :EXT, :], sbot_ref[...], lbot_ref[...], cbot_ref[...])
    acc[...] = jnp.zeros_like(acc)
    sub = lax.broadcasted_iota(I32, (8, UB), 0)

    def pair(j, carry):
        light = [[jnp.zeros((8, UB), F32) for _ in range(5)] for _ in range(4)]
        for odd in range(2):
            q = 2 * (j + 1) + odd
            strip = [None] * 5
            for w in range(WAVES):
                f = jnp.broadcast_to(f_s[w, pl.ds(q, 1), :], (8, UB))
                e = jnp.broadcast_to(e_s[w, pl.ds(q, 1), :], (8, UB))
                v = jnp.broadcast_to(a_s[w, pl.ds(q, 1), :], (8, UB))
                least, most = w + 4 * odd, w + 4 * odd + 22
                for i in range(least // 8, most // 8 + 1):
                    h = sub + 8 * i
                    add = jnp.where((h >= f) & (h < e), v, 0.0)
                    strip[i] = add if strip[i] is None else strip[i] + add
            c = jnp.broadcast_to(c_s[pl.ds(q, 1), :], (8, UB))
            for k in range(4):
                hot = c == k
                for i in range(5):
                    if strip[i] is not None:
                        light[k][i] = light[k][i] + jnp.where(hot, strip[i], 0.0)
        for k in range(4):
            for i in range(5):
                rows = pl.ds(pl.multiple_of(8 * j + 8 * i, 8), 8)
                acc[rows, UB * k:UB * k + UB] += light[k][i]
        return carry

    lax.fori_loop(0, PAIRS, pair, 0)
    image = acc[32:32 + 4 * QR, :]
    hi = image.astype(BF16)
    lo = (image - hi.astype(F32)).astype(BF16)
    n = lax.broadcasted_iota(I32, (4 * UB, 4 * UB), 0)
    x = lax.broadcasted_iota(I32, (4 * UB, 4 * UB), 1)
    spread = (4 * (n % UB) + n // UB == x).astype(F32).astype(BF16)
    out_ref[...] = jnp.dot(hi, spread, preferred_element_type=F32) + jnp.dot(lo, spread, preferred_element_type=F32)


def per_device(lyot_field, wave_scale, trace_start, trace_length, column_slot):
    x = lyot_field.reshape(PR, 2, NP // 128, 128).transpose(0, 2, 1, 3)
    vm = pl.BlockSpec(memory_space=pltpu.VMEM)
    sds = jax.ShapeDtypeStruct
    dma = pltpu.SemaphoreType.DMA
    tiles, itop, ibot, stop, sbot, ltop, lbot, ctop, cbot = pl.pallas_call(
        k1,
        out_shape=[
            sds((WAVES, QR, UB), BF16), sds((WAVES, EXTI, UB), BF16), sds((WAVES, EXTI, UB), BF16),
            sds((WAVES, EXT, UB), I32), sds((WAVES, EXT, UB), I32), sds((WAVES, EXT, UB), I32), sds((WAVES, EXT, UB), I32),
            sds((EXT, UB), I32), sds((EXT, UB), I32),
        ],
        in_specs=[pl.BlockSpec(memory_space=pltpu.SMEM), pl.BlockSpec(memory_space=pltpu.HBM)] + [pl.BlockSpec(memory_space=pltpu.HBM)] * 3,
        out_specs=[vm] * 9,
        scratch_shapes=[
            pltpu.VMEM((NP // 128, PR, 2, 128), BF16),
            pltpu.VMEM((2, 128, 512), F32), pltpu.VMEM((2, 128, 512), F32), pltpu.VMEM((2, 32, 512), F32), pltpu.VMEM((2, 32, 512), F32),
            pltpu.VMEM((2, NP, 512), BF16), pltpu.VMEM((4, 2 * PR, 128), F32),
            pltpu.VMEM((ROWS, PR, 128), BF16), pltpu.VMEM((ROWS, PR, 128), BF16),
            pltpu.VMEM((2 * QR, NQ), F32), pltpu.VMEM((WAVES, QR, UB), BF16),
            dma((ROWS,)), dma((ROWS,)), dma((WAVES,)), dma((WAVES,)), dma((2, WAVES)), dma((2, WAVES)), dma((6,)), dma((6,)), dma((NP // 128,)),
        ],
        compiler_params=pltpu.CompilerParams(collective_id=0, has_side_effects=True, vmem_limit_bytes=62 << 20),
    )(wave_scale, x, trace_start, trace_length, column_slot)
    return pl.pallas_call(
        k2,
        out_shape=sds((4 * QR, 4 * UB), F32),
        in_specs=[vm] * 12,
        out_specs=vm,
        scratch_shapes=[
            pltpu.VMEM((WAVES, QR + 2 * EXT, UB), I32), pltpu.VMEM((WAVES, QR + 2 * EXT, UB), I32),
            pltpu.VMEM((WAVES, QR + 2 * EXT, UB), F32), pltpu.VMEM((QR + 2 * EXT, UB), I32),
            pltpu.VMEM((ACC_ROWS, 4 * UB), F32),
        ],
        compiler_params=pltpu.CompilerParams(vmem_limit_bytes=16 << 20),
    )(tiles, itop, ibot, trace_start, stop, sbot, trace_length, ltop, lbot, column_slot, ctop, cbot)


def solution(mesh):
    placed = (
        P("wave", "row", None, None),
        P("wave"),
        P(None, "row", "wave"),
        P(None, "row", "wave"),
        P("row", "wave"),
    )
    return jax.shard_map(
        per_device, mesh=mesh, in_specs=placed, out_specs=P("row", "wave"), check_vma=False
    )
```

```python
import jax
import jax.numpy as jnp
from jax import lax
from jax.experimental import pallas as pl
from jax.experimental.pallas import tpu as pltpu
from jax.sharding import PartitionSpec as P

F32, BF16, I32 = jnp.float32, jnp.bfloat16, jnp.int32
MESH = pl.DeviceIdType.MESH
NP = 4096
NQ = 1024
ROWS = 16
WAVES = 8
PR = NP // ROWS
QR = NQ // ROWS
UB = NQ // WAVES
EXT = 8
EXTI = 16
HALF = PR // 2
QE = QR + 2 * EXT


def sincos_turns(turns):
    frac = turns - jnp.round(turns)
    quad = jnp.round(frac * 4.0)
    r = (frac - quad * 0.25) * 6.283185307179586
    r2 = r * r
    s = r * (1.0 + r2 * (-1.6666667e-1 + r2 * (8.3333310e-3 + r2 * (-1.9840874e-4 + r2 * 2.7525562e-6))))
    c = 1.0 + r2 * (-0.5 + r2 * (4.16666642e-2 + r2 * (-1.3888397e-3 + r2 * 2.4760495e-5)))
    odd = jnp.abs(quad) == 1.0
    cc = jnp.where(odd, s, c)
    ss = jnp.where(odd, c, s)
    cneg = (quad == 1.0) | (jnp.abs(quad) == 2.0)
    sneg = (quad == -1.0) | (jnp.abs(quad) == 2.0)
    return jnp.where(cneg, -cc, cc), jnp.where(sneg, -ss, ss)


def lens_lanes(shape, first):
    n = lax.broadcasted_iota(I32, shape, 1) + first
    i = n % 128
    k = 64 * (n // 128) + i % 64
    return k.astype(F32) - 511.5, i >= 64


def lane_sign(shape):
    return jnp.where(lax.broadcasted_iota(I32, shape, 1) < 64, 1.0, -1.0).astype(F32)


def lane_order(wave):
    n = lax.broadcasted_iota(I32, (UB, UB), 0)
    x = lax.broadcasted_iota(I32, (UB, UB), 1)
    return (n == jnp.where(wave >= WAVES // 2, UB - 1 - x, x)).astype(F32).astype(BF16)


def k1(scale_ref, x_ref, start_ref, length_ref, slot_ref,
       light_ref, begin_ref, end_ref, gain_ref, slots_ref, spread_ref,
       xv, lo_u, lo_v, hi_c, hi_s, tab0, tab1, acc, sbuf, rbuf, zacc, ibuf, start_v, length_v, slot_v,
       x_sem, own_sem, y_send, y_recv, i_send, i_recv, e_send, e_recv, t_send, t_recv):
    wave = lax.axis_index("wave")
    row = lax.axis_index("row")
    below = lax.rem(row + 1, ROWS)
    above = lax.rem(row + ROWS - 1, ROWS)
    tabs = (tab0, tab1)

    def fetch(h, c):
        return pltpu.make_async_copy(x_ref.at[pl.ds(HALF * h, HALF), c], xv.at[h, c], x_sem.at[h, c])

    for h in range(2):
        for c in range(32):
            fetch(h, c).start()

    barrier = pltpu.get_barrier_semaphore()

    def greet_row(i, carry):
        pl.semaphore_signal(barrier, inc=1, device_id=(wave, lax.rem(row + i, ROWS)), device_id_type=MESH)
        return carry

    def greet_wave(i, carry):
        pl.semaphore_signal(barrier, inc=1, device_id=(lax.rem(wave + i, WAVES), row), device_id_type=MESH)
        pl.semaphore_signal(barrier, inc=1, device_id=(lax.rem(wave + i, WAVES), below), device_id_type=MESH)
        pl.semaphore_signal(barrier, inc=1, device_id=(lax.rem(wave + i, WAVES), above), device_id_type=MESH)
        return carry

    lax.fori_loop(1, ROWS, greet_row, 0)
    lax.fori_loop(1, WAVES, greet_wave, 0)

    mid = slice(EXT, EXT + QR)
    locals_ = [
        pltpu.make_async_copy(start_ref, start_v.at[:, mid, :], own_sem.at[0]),
        pltpu.make_async_copy(length_ref, length_v.at[:, mid, :], own_sem.at[1]),
        pltpu.make_async_copy(slot_ref, slot_v.at[mid, :], own_sem.at[2]),
    ]
    for copy in locals_:
        copy.start()

    first = lax.rem(row, 2)
    s = scale_ref[0] * (1.0 / NP)

    def make_table(t):
        j = first if t == 0 else 1 - first
        y, is_sin = lens_lanes((128, 512), 512 * j)
        b = lax.broadcasted_iota(I32, (128, 512), 0).astype(F32) - 63.5
        c, sn = sincos_turns(b * y * s)
        lo_u[...] = jnp.where(is_sin, sn, c) * (1.0 / 64.0)
        lo_v[...] = jnp.where(is_sin, c, -sn) * (1.0 / 64.0)
        y, is_sin = lens_lanes((32, 512), 512 * j)
        a = lax.broadcasted_iota(I32, (32, 512), 0).astype(F32) * 128.0 - 1984.0
        c, sn = sincos_turns(a * y * s)
        hi_c[...] = c
        hi_s[...] = sn

        def make(a, carry):
            rows = pl.ds(pl.multiple_of(a * 128, 128), 128)
            tabs[t][rows, :] = (lo_u[...] * hi_c[pl.ds(a, 1), :] + lo_v[...] * hi_s[pl.ds(a, 1), :]).astype(BF16)
            return carry

        lax.fori_loop(0, 32, make, 0)

    sgn = lane_sign((HALF, 128))

    def edge_copies():
        def cp(src, dst, i, dev):
            return pltpu.make_async_remote_copy(src_ref=src, dst_ref=dst, send_sem=t_send.at[i], recv_sem=t_recv.at[i],
                                                device_id=(wave, dev), device_id_type=MESH)
        last = slice(QR - EXT, QR)
        head = slice(0, EXT)
        tail = slice(EXT + QR, QR + 2 * EXT)
        return [
            cp(start_ref.at[:, last, :], start_v.at[:, head, :], 0, below),
            cp(length_ref.at[:, last, :], length_v.at[:, head, :], 1, below),
            cp(slot_ref.at[last, :], slot_v.at[head, :], 2, below),
            cp(start_ref.at[:, head, :], start_v.at[:, tail, :], 3, above),
            cp(length_ref.at[:, head, :], length_v.at[:, tail, :], 4, above),
            cp(slot_ref.at[head, :], slot_v.at[tail, :], 5, above),
        ]

    def part(h):
        return pl.ds(pl.multiple_of(HALF * h, HALF), HALF)

    def y_copy(dest, h):
        return pltpu.make_async_remote_copy(src_ref=sbuf.at[dest, part(h)], dst_ref=rbuf.at[row, part(h)], send_sem=y_send.at[h, dest],
                                            recv_sem=y_recv.at[h, row], device_id=(wave, dest), device_id_type=MESH)

    def y_local(h):
        return pltpu.make_async_copy(sbuf.at[row, part(h)], rbuf.at[row, part(h)], y_recv.at[h, row])

    def y_arrival(src, h):
        return pltpu.make_async_remote_copy(src_ref=sbuf.at[src, part(h)], dst_ref=rbuf.at[src, part(h)], send_sem=y_send.at[h, src],
                                            recv_sem=y_recv.at[h, src], device_id=(wave, src), device_id_type=MESH)

    for t in range(2):
        make_table(t)
        j = first if t == 0 else 1 - first

        def block(h, carry):
            if t == 0:
                def arrived(c, carry):
                    fetch(h, c).wait()
                    return carry

                lax.fori_loop(0, 32, arrived, 0)
            field = jnp.concatenate([xv.at[h, c].reshape(2 * HALF, 128)[...] for c in range(32)], axis=1)
            y = jnp.dot(field, tabs[t][...], preferred_element_type=F32)
            for i in range(4):
                acc[i] = y[:, 128 * i:128 * i + 128]
            if t == 0:
                @pl.when(h == 0)
                def _():
                    pl.semaphore_wait(barrier, 36)

            def message(n, carry):
                i = lax.rem(n + row, 4)
                p = acc[i, pl.ds(0, HALF, stride=2), :]
                r = pltpu.roll(acc[i, pl.ds(1, HALF, stride=2), :], 64, 1)
                direct = 4 * j + i
                mirror = ROWS - 1 - direct
                sbuf[direct, part(h), :] = (r + sgn * p).astype(BF16)
                sbuf[mirror, part(h), :] = (p - sgn * r).astype(BF16)
                for dest in (direct, mirror):
                    @pl.when(dest != row)
                    def _():
                        y_copy(dest, h).start()

                    @pl.when(dest == row)
                    def _():
                        y_local(h).start()
                return carry

            lax.fori_loop(0, 4, message, 0)
            return carry

        lax.fori_loop(0, 2, block, 0)
        if t == 0:
            for copy in edge_copies():
                copy.start()

    for copy in locals_:
        copy.wait()
    for copy in edge_copies():
        copy.wait()
    order = lane_order(wave)
    q = lax.broadcasted_iota(I32, (QE, UB), 0)
    base = 4 * (row * QR + q - EXT) - 8 - 4 * (q % 2)

    def prepare(w, carry):
        begin = jnp.clip(start_v[w] - base, -64, 64).astype(F32).astype(BF16)
        begin = jnp.dot(begin, order, preferred_element_type=F32)
        length = jnp.dot(length_v[w].astype(F32).astype(BF16), order, preferred_element_type=F32)
        begin_ref[w] = begin.astype(I32)
        end_ref[w] = (begin + length).astype(I32)
        gain_ref[w] = 1.0 / length
        return carry

    lax.fori_loop(0, WAVES, prepare, 0)
    slots_ref[...] = jnp.dot(slot_v[...].astype(F32).astype(BF16), order, preferred_element_type=F32).astype(I32)
    n = lax.broadcasted_iota(I32, (4 * UB, 4 * UB), 0)
    x = lax.broadcasted_iota(I32, (4 * UB, 4 * UB), 1)
    lane = n % UB
    lane = jnp.where(wave >= WAVES // 2, UB - 1 - lane, lane)
    spread_ref[...] = (4 * lane + n // UB == x).astype(F32).astype(BF16)

    zacc[...] = jnp.zeros_like(zacc)
    band = row // 4
    early = jnp.where((band == 0) | (band == 3), 0, 1)

    def source(i):
        return 2 * lax.rem(row // 2 + i, 8) + jnp.where(i < 8, early, 1 - early)

    def absorb(t, carry):
        srcs = [source(2 * t + i) for i in range(2)]
        for src in srcs:
            for h in range(2):
                @pl.when(src == row)
                def _():
                    y_local(h).wait()

                @pl.when(src != row)
                def _():
                    y_arrival(src, h).wait_recv()

        for k in range(2):
            total = None
            for src in srcs:
                rows = pl.ds(pl.multiple_of(src * PR, PR), PR)
                z = lax.dot_general(rbuf[src], tabs[k][rows, :], (((0,), (0,)), ((), ())), preferred_element_type=F32)
                total = z if total is None else total + z
            zacc[k] += total
        return carry

    lax.fori_loop(0, ROWS // 2, absorb, 0)

    flip = row >= ROWS // 2
    last_rows = pl.ds(pl.multiple_of(jnp.where(flip, 0, QR - EXTI), EXTI), EXTI)
    first_rows = pl.ds(pl.multiple_of(jnp.where(flip, QR - EXTI, 0), EXTI), EXTI)
    main = pl.ds(EXTI, QR)
    headi = pl.ds(0, EXTI)
    taili = pl.ds(EXTI + QR, EXTI)

    def i_copy(dest):
        return pltpu.make_async_remote_copy(src_ref=ibuf.at[dest], dst_ref=light_ref.at[wave, main, :], send_sem=i_send.at[dest],
                                            recv_sem=i_recv.at[wave], device_id=(dest, row), device_id_type=MESH)

    def top_copy(dest):
        return pltpu.make_async_remote_copy(src_ref=ibuf.at[dest, last_rows, :], dst_ref=light_ref.at[wave, headi, :], send_sem=e_send.at[0, dest],
                                            recv_sem=e_recv.at[0, wave], device_id=(dest, below), device_id_type=MESH)

    def bot_copy(dest):
        return pltpu.make_async_remote_copy(src_ref=ibuf.at[dest, first_rows, :], dst_ref=light_ref.at[wave, taili, :], send_sem=e_send.at[1, dest],
                                            recv_sem=e_recv.at[1, wave], device_id=(dest, above), device_id_type=MESH)

    def own():
        return pltpu.make_async_copy(ibuf.at[wave], light_ref.at[wave, main, :], i_recv.at[wave])

    sgz = lane_sign((QR, 128))
    low = lax.broadcasted_iota(I32, (QR, 128), 1) < 64

    def intensities(m, carry):
        k = jnp.where(first == m // 2, 0, 1)
        direct, mirror = [], []
        for blk in range(2):
            cols = pl.ds(pl.multiple_of(256 * lax.rem(m, 2) + 128 * blk, 128), 128)
            p = zacc[k, 0:QR, cols]
            r = pltpu.roll(zacc[k, QR:2 * QR, cols], 64, 1)
            z1 = r + sgz * p
            z2 = p - sgz * r
            z1 = z1 * z1
            z2 = z2 * z2
            direct.append(z1 + pltpu.roll(z1, 64, 1))
            mirror.append(z2 + pltpu.roll(z2, 64, 1))
        ibuf[m] = jnp.where(low, direct[0], direct[1]).astype(BF16)
        ibuf[WAVES - 1 - m] = jnp.where(low, mirror[0], mirror[1]).astype(BF16)
        for dest in (m, WAVES - 1 - m):
            top_copy(dest).start()
            bot_copy(dest).start()

            @pl.when(dest != wave)
            def _():
                i_copy(dest).start()

            @pl.when(dest == wave)
            def _():
                own().start()
        return carry

    lax.fori_loop(0, 4, intensities, 0)

    def drain(t, carry):
        for h in range(2):
            y_copy(lax.rem(row + t, ROWS), h).wait_send()
        return carry

    lax.fori_loop(1, ROWS, drain, 0)

    def i_arrival(src):
        return pltpu.make_async_remote_copy(src_ref=ibuf.at[src], dst_ref=light_ref.at[src, main, :], send_sem=i_send.at[src],
                                            recv_sem=i_recv.at[src], device_id=(src, row), device_id_type=MESH)

    def top_arrival(src):
        return pltpu.make_async_remote_copy(src_ref=ibuf.at[src, last_rows, :], dst_ref=light_ref.at[src, headi, :], send_sem=e_send.at[0, src],
                                            recv_sem=e_recv.at[0, src], device_id=(src, below), device_id_type=MESH)

    def bot_arrival(src):
        return pltpu.make_async_remote_copy(src_ref=ibuf.at[src, first_rows, :], dst_ref=light_ref.at[src, taili, :], send_sem=e_send.at[1, src],
                                            recv_sem=e_recv.at[1, src], device_id=(src, above), device_id_type=MESH)

    def finish(t, carry):
        src = lax.rem(wave + t, WAVES)

        @pl.when(t != 0)
        def _():
            i_arrival(src).wait()

        @pl.when(t == 0)
        def _():
            own().wait()
        top_arrival(src).wait()
        bot_arrival(src).wait()
        return carry

    lax.fori_loop(0, WAVES, finish, 0)


PAIRS = 36
ACC_ROWS = 8 * PAIRS + 40


def k2(light_ref, begin_ref, end_ref, gain_ref, slots_ref, spread_ref, out_ref, lf, acc):
    row = lax.axis_index("row")
    flip = row >= ROWS // 2
    flip_above = lax.rem(row + ROWS - 1, ROWS) >= ROWS // 2
    flip_below = lax.rem(row + 1, ROWS) >= ROWS // 2
    lf[...] = light_ref[...].astype(F32)
    acc[...] = jnp.zeros_like(acc)
    sub = lax.broadcasted_iota(I32, (8, UB), 0)

    def held(q):
        n = q - EXT
        top = jnp.where(flip_above, 7 - q, 8 + q)
        mid = EXTI + jnp.where(flip, QR - 1 - n, n)
        n = q - EXT - QR
        bot = EXTI + QR + jnp.where(flip_below, EXTI - 1 - n, n)
        return jnp.where(q < EXT, top, jnp.where(q < EXT + QR, mid, bot))

    def pair(j, carry):
        light = [[jnp.zeros((8, UB), F32) for _ in range(5)] for _ in range(4)]
        for odd in range(2):
            q = 2 * (j + 1) + odd
            at = held(q)
            strip = [None] * 5
            for w in range(WAVES):
                f = jnp.broadcast_to(begin_ref[w, pl.ds(q, 1), :], (8, UB))
                e = jnp.broadcast_to(end_ref[w, pl.ds(q, 1), :], (8, UB))
                v = jnp.broadcast_to(lf[w, pl.ds(at, 1), :] * gain_ref[w, pl.ds(q, 1), :], (8, UB))
                least, most = w + 4 * odd, w + 4 * odd + 22
                for i in range(least // 8, most // 8 + 1):
                    h = sub + 8 * i
                    add = jnp.where((h >= f) & (h < e), v, 0.0)
                    strip[i] = add if strip[i] is None else strip[i] + add
            c = jnp.broadcast_to(slots_ref[pl.ds(q, 1), :], (8, UB))
            for k in range(4):
                hot = c == k
                for i in range(5):
                    if strip[i] is not None:
                        light[k][i] = light[k][i] + jnp.where(hot, strip[i], 0.0)
        for k in range(4):
            for i in range(5):
                rows = pl.ds(pl.multiple_of(8 * j + 8 * i, 8), 8)
                acc[rows, UB * k:UB * k + UB] += light[k][i]
        return carry

    lax.fori_loop(0, PAIRS, pair, 0)
    image = acc[32:32 + 4 * QR, :]
    hi = image.astype(BF16)
    lo = (image - hi.astype(F32)).astype(BF16)
    spread = spread_ref[...]
    out_ref[...] = jnp.dot(hi, spread, preferred_element_type=F32) + jnp.dot(lo, spread, preferred_element_type=F32)


def per_device(lyot_field, wave_scale, trace_start, trace_length, column_slot):
    x = lyot_field.reshape(PR, 2, NP // 128, 128).transpose(0, 2, 1, 3)
    vm = pl.BlockSpec(memory_space=pltpu.VMEM)
    hbm = pl.BlockSpec(memory_space=pltpu.HBM)
    sds = jax.ShapeDtypeStruct
    dma = pltpu.SemaphoreType.DMA
    outs = pl.pallas_call(
        k1,
        out_shape=[
            sds((WAVES, QR + 2 * EXTI, UB), BF16),
            sds((WAVES, QE, UB), I32), sds((WAVES, QE, UB), I32), sds((WAVES, QE, UB), F32), sds((QE, UB), I32),
            sds((4 * UB, 4 * UB), BF16),
        ],
        in_specs=[pl.BlockSpec(memory_space=pltpu.SMEM), hbm, hbm, hbm, hbm],
        out_specs=[vm] * 6,
        scratch_shapes=[
            pltpu.VMEM((2, NP // 128, HALF, 2, 128), BF16),
            pltpu.VMEM((128, 512), F32), pltpu.VMEM((128, 512), F32), pltpu.VMEM((32, 512), F32), pltpu.VMEM((32, 512), F32),
            pltpu.VMEM((NP, 512), BF16), pltpu.VMEM((NP, 512), BF16), pltpu.VMEM((4, 2 * HALF, 128), F32),
            pltpu.VMEM((ROWS, PR, 128), BF16), pltpu.VMEM((ROWS, PR, 128), BF16),
            pltpu.VMEM((2, 2 * QR, 512), F32), pltpu.VMEM((WAVES, QR, UB), BF16),
            pltpu.VMEM((WAVES, QE, UB), I32), pltpu.VMEM((WAVES, QE, UB), I32), pltpu.VMEM((QE, UB), I32),
            dma((2, NP // 128)), dma((3,)), dma((2, ROWS)), dma((2, ROWS)), dma((WAVES,)), dma((WAVES,)),
            dma((2, WAVES)), dma((2, WAVES)), dma((6,)), dma((6,)),
        ],
        compiler_params=pltpu.CompilerParams(collective_id=0, has_side_effects=True, vmem_limit_bytes=50 << 20),
    )(wave_scale, x, trace_start, trace_length, column_slot)
    return pl.pallas_call(
        k2,
        out_shape=sds((4 * QR, 4 * UB), F32),
        in_specs=[vm] * 6,
        out_specs=vm,
        scratch_shapes=[pltpu.VMEM((WAVES, QR + 2 * EXTI, UB), F32), pltpu.VMEM((ACC_ROWS, 4 * UB), F32)],
        compiler_params=pltpu.CompilerParams(vmem_limit_bytes=16 << 20),
    )(*outs)


def solution(mesh):
    placed = (
        P("wave", "row", None, None),
        P("wave"),
        P(None, "row", "wave"),
        P(None, "row", "wave"),
        P("row", "wave"),
    )
    return jax.shard_map(
        per_device, mesh=mesh, in_specs=placed, out_specs=P("row", "wave"), check_vma=False
    )
```

```python
import jax
import jax.numpy as jnp
from jax import lax
from jax.experimental import pallas as pl
from jax.experimental.pallas import tpu as pltpu
from jax.sharding import PartitionSpec as P

F32, BF16, I32 = jnp.float32, jnp.bfloat16, jnp.int32
MESH = pl.DeviceIdType.MESH
NP = 4096
NQ = 1024
ROWS = 16
WAVES = 8
PR = NP // ROWS
QR = NQ // ROWS
UB = NQ // WAVES
EXT = 8
EXTI = 16
HALF = PR // 2
QE = QR + 2 * EXT
PAIRS = 36
ACC_ROWS = 8 * PAIRS + 40


def sincos_turns(turns):
    frac = turns - jnp.round(turns)
    quad = jnp.round(frac * 4.0)
    r = (frac - quad * 0.25) * 6.283185307179586
    r2 = r * r
    s = r * (1.0 + r2 * (-1.6666667e-1 + r2 * (8.3333310e-3 + r2 * (-1.9840874e-4 + r2 * 2.7525562e-6))))
    c = 1.0 + r2 * (-0.5 + r2 * (4.16666642e-2 + r2 * (-1.3888397e-3 + r2 * 2.4760495e-5)))
    odd = jnp.abs(quad) == 1.0
    cc = jnp.where(odd, s, c)
    ss = jnp.where(odd, c, s)
    cneg = (quad == 1.0) | (jnp.abs(quad) == 2.0)
    sneg = (quad == -1.0) | (jnp.abs(quad) == 2.0)
    return jnp.where(cneg, -cc, cc), jnp.where(sneg, -ss, ss)


def lens_lanes(shape, first):
    n = lax.broadcasted_iota(I32, shape, 1) + first
    i = n % 128
    k = 64 * (n // 128) + i % 64
    return k.astype(F32) - 511.5, i >= 64


def lane_sign(shape):
    return jnp.where(lax.broadcasted_iota(I32, shape, 1) < 64, 1.0, -1.0).astype(F32)


def lane_order(wave):
    n = lax.broadcasted_iota(I32, (UB, UB), 0)
    x = lax.broadcasted_iota(I32, (UB, UB), 1)
    return (n == jnp.where(wave >= WAVES // 2, UB - 1 - x, x)).astype(F32).astype(BF16)


def window(w, odd):
    return range((w + 4 * odd) // 8, (w + 4 * odd + 22) // 8 + 1)


def k1(scale_ref, x_ref, start_ref, length_ref, slot_ref,
       out_ref,
       light_ref, slots_ref, spread_ref, mask, lf, image,
       xv, lo_u, lo_v, hi_c, hi_s, tab0, tab1, acc, sbuf, rbuf, zacc, ibuf, start_v, length_v, slot_v, begin_v, count_v, gain_v,
       x_sem, own_sem, y_send, y_recv, i_send, i_recv, e_send, e_recv, t_send, t_recv):
    wave = lax.axis_index("wave")
    row = lax.axis_index("row")
    below = lax.rem(row + 1, ROWS)
    above = lax.rem(row + ROWS - 1, ROWS)
    tabs = (tab0, tab1)

    def fetch(h, c):
        return pltpu.make_async_copy(x_ref.at[pl.ds(HALF * h, HALF), c], xv.at[h, c], x_sem.at[h, c])

    for h in range(2):
        for c in range(32):
            fetch(h, c).start()

    barrier = pltpu.get_barrier_semaphore()

    def greet_row(i, carry):
        pl.semaphore_signal(barrier, inc=1, device_id=(wave, lax.rem(row + i, ROWS)), device_id_type=MESH)
        return carry

    def greet_wave(i, carry):
        pl.semaphore_signal(barrier, inc=1, device_id=(lax.rem(wave + i, WAVES), row), device_id_type=MESH)
        pl.semaphore_signal(barrier, inc=1, device_id=(lax.rem(wave + i, WAVES), below), device_id_type=MESH)
        pl.semaphore_signal(barrier, inc=1, device_id=(lax.rem(wave + i, WAVES), above), device_id_type=MESH)
        return carry

    lax.fori_loop(1, ROWS, greet_row, 0)
    lax.fori_loop(1, WAVES, greet_wave, 0)

    mid = slice(EXT, EXT + QR)
    locals_ = [
        pltpu.make_async_copy(start_ref, start_v.at[:, mid, :], own_sem.at[0]),
        pltpu.make_async_copy(length_ref, length_v.at[:, mid, :], own_sem.at[1]),
        pltpu.make_async_copy(slot_ref, slot_v.at[mid, :], own_sem.at[2]),
    ]
    for copy in locals_:
        copy.start()

    first = lax.rem(row, 2)
    s = scale_ref[0] * (1.0 / NP)

    def make_table(t):
        j = first if t == 0 else 1 - first
        y, is_sin = lens_lanes((128, 512), 512 * j)
        b = lax.broadcasted_iota(I32, (128, 512), 0).astype(F32) - 63.5
        c, sn = sincos_turns(b * y * s)
        lo_u[...] = jnp.where(is_sin, sn, c) * (1.0 / 64.0)
        lo_v[...] = jnp.where(is_sin, c, -sn) * (1.0 / 64.0)
        y, is_sin = lens_lanes((32, 512), 512 * j)
        a = lax.broadcasted_iota(I32, (32, 512), 0).astype(F32) * 128.0 - 1984.0
        c, sn = sincos_turns(a * y * s)
        hi_c[...] = c
        hi_s[...] = sn

        def make(a, carry):
            rows = pl.ds(pl.multiple_of(a * 128, 128), 128)
            tabs[t][rows, :] = (lo_u[...] * hi_c[pl.ds(a, 1), :] + lo_v[...] * hi_s[pl.ds(a, 1), :]).astype(BF16)
            return carry

        lax.fori_loop(0, 32, make, 0)

    sgn = lane_sign((HALF, 128))

    def edge_copies():
        def cp(src, dst, i, dev):
            return pltpu.make_async_remote_copy(src_ref=src, dst_ref=dst, send_sem=t_send.at[i], recv_sem=t_recv.at[i],
                                                device_id=(wave, dev), device_id_type=MESH)
        last = slice(QR - EXT, QR)
        head = slice(0, EXT)
        tail = slice(EXT + QR, QR + 2 * EXT)
        return [
            cp(start_ref.at[:, last, :], start_v.at[:, head, :], 0, below),
            cp(length_ref.at[:, last, :], length_v.at[:, head, :], 1, below),
            cp(slot_ref.at[last, :], slot_v.at[head, :], 2, below),
            cp(start_ref.at[:, head, :], start_v.at[:, tail, :], 3, above),
            cp(length_ref.at[:, head, :], length_v.at[:, tail, :], 4, above),
            cp(slot_ref.at[head, :], slot_v.at[tail, :], 5, above),
        ]

    def part(h):
        return pl.ds(pl.multiple_of(HALF * h, HALF), HALF)

    def y_copy(dest, h):
        return pltpu.make_async_remote_copy(src_ref=sbuf.at[dest, part(h)], dst_ref=rbuf.at[row, part(h)], send_sem=y_send.at[h, dest],
                                            recv_sem=y_recv.at[h, row], device_id=(wave, dest), device_id_type=MESH)

    def y_local(h):
        return pltpu.make_async_copy(sbuf.at[row, part(h)], rbuf.at[row, part(h)], y_recv.at[h, row])

    def y_arrival(src, h):
        return pltpu.make_async_remote_copy(src_ref=sbuf.at[src, part(h)], dst_ref=rbuf.at[src, part(h)], send_sem=y_send.at[h, src],
                                            recv_sem=y_recv.at[h, src], device_id=(wave, src), device_id_type=MESH)

    for t in range(2):
        make_table(t)
        j = first if t == 0 else 1 - first

        def block(h, carry):
            if t == 0:
                def arrived(c, carry):
                    fetch(h, c).wait()
                    return carry

                lax.fori_loop(0, 32, arrived, 0)
            field = jnp.concatenate([xv.at[h, c].reshape(2 * HALF, 128)[...] for c in range(32)], axis=1)
            y = jnp.dot(field, tabs[t][...], preferred_element_type=F32)
            for i in range(4):
                acc[i] = y[:, 128 * i:128 * i + 128]
            if t == 0:
                @pl.when(h == 0)
                def _():
                    pl.semaphore_wait(barrier, 36)

            def message(n, carry):
                i = lax.rem(n + row, 4)
                p = acc[i, pl.ds(0, HALF, stride=2), :]
                r = pltpu.roll(acc[i, pl.ds(1, HALF, stride=2), :], 64, 1)
                direct = 4 * j + i
                mirror = ROWS - 1 - direct
                sbuf[direct, part(h), :] = (r + sgn * p).astype(BF16)
                sbuf[mirror, part(h), :] = (p - sgn * r).astype(BF16)
                for dest in (direct, mirror):
                    @pl.when(dest != row)
                    def _():
                        y_copy(dest, h).start()

                    @pl.when(dest == row)
                    def _():
                        y_local(h).start()
                return carry

            lax.fori_loop(0, 4, message, 0)
            return carry

        lax.fori_loop(0, 2, block, 0)
        if t == 0:
            for copy in edge_copies():
                copy.start()

    zacc[...] = jnp.zeros_like(zacc)
    band = row // 4
    early = jnp.where((band == 0) | (band == 3), 0, 1)

    def source(i):
        return 2 * lax.rem(row // 2 + i, 8) + jnp.where(i < 8, early, 1 - early)

    def absorb(t, carry):
        srcs = [source(2 * t + i) for i in range(2)]
        for src in srcs:
            for h in range(2):
                @pl.when(src == row)
                def _():
                    y_local(h).wait()

                @pl.when(src != row)
                def _():
                    y_arrival(src, h).wait_recv()

        for k in range(2):
            total = None
            for src in srcs:
                rows = pl.ds(pl.multiple_of(src * PR, PR), PR)
                z = lax.dot_general(rbuf[src], tabs[k][rows, :], (((0,), (0,)), ((), ())), preferred_element_type=F32)
                total = z if total is None else total + z
            zacc[k] += total
        return carry

    lax.fori_loop(0, ROWS // 2, absorb, 0)

    flip = row >= ROWS // 2
    last_rows = pl.ds(pl.multiple_of(jnp.where(flip, 0, QR - EXTI), EXTI), EXTI)
    first_rows = pl.ds(pl.multiple_of(jnp.where(flip, QR - EXTI, 0), EXTI), EXTI)
    main = pl.ds(EXTI, QR)
    headi = pl.ds(0, EXTI)
    taili = pl.ds(EXTI + QR, EXTI)

    def i_copy(dest):
        return pltpu.make_async_remote_copy(src_ref=ibuf.at[dest], dst_ref=light_ref.at[wave, main, :], send_sem=i_send.at[dest],
                                            recv_sem=i_recv.at[wave], device_id=(dest, row), device_id_type=MESH)

    def top_copy(dest):
        return pltpu.make_async_remote_copy(src_ref=ibuf.at[dest, last_rows, :], dst_ref=light_ref.at[wave, headi, :], send_sem=e_send.at[0, dest],
                                            recv_sem=e_recv.at[0, wave], device_id=(dest, below), device_id_type=MESH)

    def bot_copy(dest):
        return pltpu.make_async_remote_copy(src_ref=ibuf.at[dest, first_rows, :], dst_ref=light_ref.at[wave, taili, :], send_sem=e_send.at[1, dest],
                                            recv_sem=e_recv.at[1, wave], device_id=(dest, above), device_id_type=MESH)

    def own():
        return pltpu.make_async_copy(ibuf.at[wave], light_ref.at[wave, main, :], i_recv.at[wave])

    sgz = lane_sign((QR, 128))
    low = lax.broadcasted_iota(I32, (QR, 128), 1) < 64

    def intensities(m, carry):
        k = jnp.where(first == m // 2, 0, 1)
        direct, mirror = [], []
        for blk in range(2):
            cols = pl.ds(pl.multiple_of(256 * lax.rem(m, 2) + 128 * blk, 128), 128)
            p = zacc[k, 0:QR, cols]
            r = pltpu.roll(zacc[k, QR:2 * QR, cols], 64, 1)
            z1 = r + sgz * p
            z2 = p - sgz * r
            z1 = z1 * z1
            z2 = z2 * z2
            direct.append(z1 + pltpu.roll(z1, 64, 1))
            mirror.append(z2 + pltpu.roll(z2, 64, 1))
        ibuf[m] = jnp.where(low, direct[0], direct[1]).astype(BF16)
        ibuf[WAVES - 1 - m] = jnp.where(low, mirror[0], mirror[1]).astype(BF16)
        for dest in (m, WAVES - 1 - m):
            top_copy(dest).start()
            bot_copy(dest).start()

            @pl.when(dest != wave)
            def _():
                i_copy(dest).start()

            @pl.when(dest == wave)
            def _():
                own().start()
        return carry

    lax.fori_loop(0, 4, intensities, 0)

    for copy in locals_:
        copy.wait()
    for copy in edge_copies():
        copy.wait()
    order = lane_order(wave)
    q = lax.broadcasted_iota(I32, (QE, UB), 0)
    base = 4 * (row * QR + q - EXT) - 8 - 4 * (q % 2)

    def prepare(w, carry):
        begin = jnp.clip(start_v[w] - base, -64, 64).astype(F32).astype(BF16)
        begin = jnp.dot(begin, order, preferred_element_type=F32)
        length = jnp.dot(length_v[w].astype(F32).astype(BF16), order, preferred_element_type=F32)
        begin_v[w] = begin.astype(I32)
        count_v[w] = length.astype(I32)
        gain_v[w] = 1.0 / length
        return carry

    lax.fori_loop(0, WAVES, prepare, 0)
    slots_ref[...] = jnp.dot(slot_v[...].astype(F32).astype(BF16), order, preferred_element_type=F32).astype(I32)
    n = lax.broadcasted_iota(I32, (4 * UB, 4 * UB), 0)
    x = lax.broadcasted_iota(I32, (4 * UB, 4 * UB), 1)
    lane = n % UB
    lane = jnp.where(wave >= WAVES // 2, UB - 1 - lane, lane)
    spread_ref[...] = (4 * lane + n // UB == x).astype(F32).astype(BF16)
    sub = lax.broadcasted_iota(I32, (8, UB), 0)

    def make_masks(j, carry):
        for odd in range(2):
            q = 2 * (j + 1) + odd
            for w in range(WAVES):
                f = jnp.broadcast_to(begin_v[w, pl.ds(q, 1), :], (8, UB))
                e = jnp.broadcast_to(count_v[w, pl.ds(q, 1), :], (8, UB)).astype(jnp.uint32)
                g = jnp.broadcast_to(gain_v[w, pl.ds(q, 1), :], (8, UB))
                for k, i in enumerate(window(w, odd)):
                    mask[w, j, odd, 8 * k:8 * k + 8, :] = jnp.where((sub + 8 * i - f).astype(jnp.uint32) < e, g, 0.0)
        return carry

    lax.fori_loop(0, PAIRS, make_masks, 0)
    image[...] = jnp.zeros_like(image)

    def drain(t, carry):
        for h in range(2):
            y_copy(lax.rem(row + t, ROWS), h).wait_send()
        return carry

    lax.fori_loop(1, ROWS, drain, 0)

    def i_arrival(src):
        return pltpu.make_async_remote_copy(src_ref=ibuf.at[src], dst_ref=light_ref.at[src, main, :], send_sem=i_send.at[src],
                                            recv_sem=i_recv.at[src], device_id=(src, row), device_id_type=MESH)

    def top_arrival(src):
        return pltpu.make_async_remote_copy(src_ref=ibuf.at[src, last_rows, :], dst_ref=light_ref.at[src, headi, :], send_sem=e_send.at[0, src],
                                            recv_sem=e_recv.at[0, src], device_id=(src, below), device_id_type=MESH)

    def bot_arrival(src):
        return pltpu.make_async_remote_copy(src_ref=ibuf.at[src, first_rows, :], dst_ref=light_ref.at[src, taili, :], send_sem=e_send.at[1, src],
                                            recv_sem=e_recv.at[1, src], device_id=(src, above), device_id_type=MESH)

    def finish(t, carry):
        src = lax.rem(wave + t, WAVES)

        @pl.when(t != 0)
        def _():
            i_arrival(src).wait()

        @pl.when(t == 0)
        def _():
            own().wait()
        top_arrival(src).wait()
        bot_arrival(src).wait()
        return carry

    lax.fori_loop(0, WAVES, finish, 0)
    flip_above = above >= ROWS // 2
    flip_below = below >= ROWS // 2
    lf[...] = light_ref[...].astype(F32)

    def held(q):
        n = q - EXT
        top = jnp.where(flip_above, 7 - q, 8 + q)
        mid_at = EXTI + jnp.where(flip, QR - 1 - n, n)
        n = q - EXT - QR
        bot = EXTI + QR + jnp.where(flip_below, EXTI - 1 - n, n)
        return jnp.where(q < EXT, top, jnp.where(q < EXT + QR, mid_at, bot))

    def pair(j, carry):
        light = [[None] * 5 for _ in range(4)]
        for odd in range(2):
            q = 2 * (j + 1) + odd
            at = held(q)
            strip = [None] * 5
            for w in range(WAVES):
                v = jnp.broadcast_to(lf[w, pl.ds(at, 1), :], (8, UB))
                for k, i in enumerate(window(w, odd)):
                    add = mask[w, j, odd, 8 * k:8 * k + 8, :] * v
                    strip[i] = add if strip[i] is None else strip[i] + add
            c = jnp.broadcast_to(slots_ref[pl.ds(q, 1), :], (8, UB))
            for k in range(4):
                hot = c == k
                for i in range(5):
                    if strip[i] is not None:
                        add = jnp.where(hot, strip[i], 0.0)
                        light[k][i] = add if light[k][i] is None else light[k][i] + add
        for k in range(4):
            for i in range(5):
                rows = pl.ds(pl.multiple_of(8 * j + 8 * i, 8), 8)
                image[rows, UB * k:UB * k + UB] += light[k][i]
        return carry

    lax.fori_loop(0, PAIRS, pair, 0)
    whole = image[32:32 + 4 * QR, :]
    hi = whole.astype(BF16)
    lo = (whole - hi.astype(F32)).astype(BF16)
    spread = spread_ref[...]
    out_ref[...] = jnp.dot(hi, spread, preferred_element_type=F32) + jnp.dot(lo, spread, preferred_element_type=F32)


def per_device(lyot_field, wave_scale, trace_start, trace_length, column_slot):
    x = lyot_field.reshape(PR, 2, NP // 128, 128).transpose(0, 2, 1, 3)
    vm = pl.BlockSpec(memory_space=pltpu.VMEM)
    hbm = pl.BlockSpec(memory_space=pltpu.HBM)
    dma = pltpu.SemaphoreType.DMA
    return pl.pallas_call(
        k1,
        out_shape=jax.ShapeDtypeStruct((4 * QR, 4 * UB), F32),
        in_specs=[pl.BlockSpec(memory_space=pltpu.SMEM), hbm, hbm, hbm, hbm],
        out_specs=vm,
        scratch_shapes=[
            pltpu.VMEM((WAVES, QR + 2 * EXTI, UB), BF16), pltpu.VMEM((QE, UB), I32), pltpu.VMEM((4 * UB, 4 * UB), BF16),
            pltpu.VMEM((WAVES, PAIRS, 2, 32, UB), F32), pltpu.VMEM((WAVES, QR + 2 * EXTI, UB), F32), pltpu.VMEM((ACC_ROWS, 4 * UB), F32),
            pltpu.VMEM((2, NP // 128, HALF, 2, 128), BF16),
            pltpu.VMEM((128, 512), F32), pltpu.VMEM((128, 512), F32), pltpu.VMEM((32, 512), F32), pltpu.VMEM((32, 512), F32),
            pltpu.VMEM((NP, 512), BF16), pltpu.VMEM((NP, 512), BF16), pltpu.VMEM((4, 2 * HALF, 128), F32),
            pltpu.VMEM((ROWS, PR, 128), BF16), pltpu.VMEM((ROWS, PR, 128), BF16),
            pltpu.VMEM((2, 2 * QR, 512), F32), pltpu.VMEM((WAVES, QR, UB), BF16),
            pltpu.VMEM((WAVES, QE, UB), I32), pltpu.VMEM((WAVES, QE, UB), I32), pltpu.VMEM((QE, UB), I32),
            pltpu.VMEM((WAVES, QE, UB), I32), pltpu.VMEM((WAVES, QE, UB), I32), pltpu.VMEM((WAVES, QE, UB), F32),
            dma((2, NP // 128)), dma((3,)), dma((2, ROWS)), dma((2, ROWS)), dma((WAVES,)), dma((WAVES,)),
            dma((2, WAVES)), dma((2, WAVES)), dma((6,)), dma((6,)),
        ],
        compiler_params=pltpu.CompilerParams(collective_id=0, has_side_effects=True, vmem_limit_bytes=62 << 20),
    )(wave_scale, x, trace_start, trace_length, column_slot)


def solution(mesh):
    placed = (
        P("wave", "row", None, None),
        P("wave"),
        P(None, "row", "wave"),
        P(None, "row", "wave"),
        P("row", "wave"),
    )
    return jax.shard_map(
        per_device, mesh=mesh, in_specs=placed, out_specs=P("row", "wave"), check_vma=False
    )
```

```python
import jax
import jax.numpy as jnp
from jax import lax
from jax.experimental import pallas as pl
from jax.experimental.pallas import tpu as pltpu
from jax.sharding import PartitionSpec as P

F32, BF16, I32 = jnp.float32, jnp.bfloat16, jnp.int32
MESH = pl.DeviceIdType.MESH
NP = 4096
NQ = 1024
ROWS = 16
WAVES = 8
PR = NP // ROWS
QR = NQ // ROWS
UB = NQ // WAVES
EXT = 8
EXTI = 16
HALF = PR // 2
QE = QR + 2 * EXT
PAIRS = 36
ACC_ROWS = 8 * PAIRS + 40


def sincos_turns(turns):
    frac = turns - jnp.round(turns)
    quad = jnp.round(frac * 4.0)
    r = (frac - quad * 0.25) * 6.283185307179586
    r2 = r * r
    s = r * (1.0 + r2 * (-1.6666667e-1 + r2 * (8.3333310e-3 + r2 * (-1.9840874e-4 + r2 * 2.7525562e-6))))
    c = 1.0 + r2 * (-0.5 + r2 * (4.16666642e-2 + r2 * (-1.3888397e-3 + r2 * 2.4760495e-5)))
    odd = jnp.abs(quad) == 1.0
    cc = jnp.where(odd, s, c)
    ss = jnp.where(odd, c, s)
    cneg = (quad == 1.0) | (jnp.abs(quad) == 2.0)
    sneg = (quad == -1.0) | (jnp.abs(quad) == 2.0)
    return jnp.where(cneg, -cc, cc), jnp.where(sneg, -ss, ss)


def lens_lanes(shape, half):
    n = lax.broadcasted_iota(I32, shape, 1)
    i = n % 128
    k = 64 * (2 * (n // 128) + half) + i % 64
    return k.astype(F32) - 511.5, i >= 64


def lane_sign(shape):
    return jnp.where(lax.broadcasted_iota(I32, shape, 1) < 64, 1.0, -1.0).astype(F32)


def lane_order(wave):
    n = lax.broadcasted_iota(I32, (UB, UB), 0)
    x = lax.broadcasted_iota(I32, (UB, UB), 1)
    return (n == jnp.where(wave >= WAVES // 2, UB - 1 - x, x)).astype(F32).astype(BF16)


def window(w, odd):
    return range((w + 4 * odd) // 8, (w + 4 * odd + 22) // 8 + 1)


def k1(scale_ref, x_ref, start_ref, length_ref, slot_ref,
       out_ref,
       light_ref, slots_ref, spread_ref, mask, lf, image,
       xv, lo_u, lo_v, hi_c, hi_s, tab0, tab1, acc, sbuf, rbuf, zacc, ibuf, start_v, length_v, slot_v, begin_v, count_v, gain_v,
       x_sem, own_sem, y_send, y_recv, i_send, i_recv, e_send, e_recv, t_send, t_recv):
    wave = lax.axis_index("wave")
    row = lax.axis_index("row")
    below = lax.rem(row + 1, ROWS)
    above = lax.rem(row + ROWS - 1, ROWS)
    tabs = (tab0, tab1)

    def fetch(h, c):
        return pltpu.make_async_copy(x_ref.at[pl.ds(HALF * h, HALF), c], xv.at[h, c], x_sem.at[h, c])

    for h in range(2):
        for c in range(32):
            fetch(h, c).start()

    barrier = pltpu.get_barrier_semaphore()

    def greet_row(i, carry):
        pl.semaphore_signal(barrier, inc=1, device_id=(wave, lax.rem(row + i, ROWS)), device_id_type=MESH)
        return carry

    def greet_wave(i, carry):
        pl.semaphore_signal(barrier, inc=1, device_id=(lax.rem(wave + i, WAVES), row), device_id_type=MESH)
        pl.semaphore_signal(barrier, inc=1, device_id=(lax.rem(wave + i, WAVES), below), device_id_type=MESH)
        pl.semaphore_signal(barrier, inc=1, device_id=(lax.rem(wave + i, WAVES), above), device_id_type=MESH)
        return carry

    lax.fori_loop(1, ROWS, greet_row, 0)
    lax.fori_loop(1, WAVES, greet_wave, 0)

    mid = slice(EXT, EXT + QR)
    locals_ = [
        pltpu.make_async_copy(start_ref, start_v.at[:, mid, :], own_sem.at[0]),
        pltpu.make_async_copy(length_ref, length_v.at[:, mid, :], own_sem.at[1]),
        pltpu.make_async_copy(slot_ref, slot_v.at[mid, :], own_sem.at[2]),
    ]
    for copy in locals_:
        copy.start()

    first = lax.rem(row + row // 4, 2)
    s = scale_ref[0] * (1.0 / NP)

    def make_table(t):
        j = first if t == 0 else 1 - first
        y, is_sin = lens_lanes((128, 512), j)
        b = lax.broadcasted_iota(I32, (128, 512), 0).astype(F32) - 63.5
        c, sn = sincos_turns(b * y * s)
        lo_u[...] = jnp.where(is_sin, sn, c) * (1.0 / 64.0)
        lo_v[...] = jnp.where(is_sin, c, -sn) * (1.0 / 64.0)
        y, is_sin = lens_lanes((32, 512), j)
        a = lax.broadcasted_iota(I32, (32, 512), 0).astype(F32) * 128.0 - 1984.0
        c, sn = sincos_turns(a * y * s)
        hi_c[...] = c
        hi_s[...] = sn

        def make(a, carry):
            rows = pl.ds(pl.multiple_of(a * 128, 128), 128)
            tabs[t][rows, :] = (lo_u[...] * hi_c[pl.ds(a, 1), :] + lo_v[...] * hi_s[pl.ds(a, 1), :]).astype(BF16)
            return carry

        lax.fori_loop(0, 32, make, 0)

    sgn = lane_sign((HALF, 128))

    def edge_copies():
        def cp(src, dst, i, dev):
            return pltpu.make_async_remote_copy(src_ref=src, dst_ref=dst, send_sem=t_send.at[i], recv_sem=t_recv.at[i],
                                                device_id=(wave, dev), device_id_type=MESH)
        last = slice(QR - EXT, QR)
        head = slice(0, EXT)
        tail = slice(EXT + QR, QR + 2 * EXT)
        return [
            cp(start_ref.at[:, last, :], start_v.at[:, head, :], 0, below),
            cp(length_ref.at[:, last, :], length_v.at[:, head, :], 1, below),
            cp(slot_ref.at[last, :], slot_v.at[head, :], 2, below),
            cp(start_ref.at[:, head, :], start_v.at[:, tail, :], 3, above),
            cp(length_ref.at[:, head, :], length_v.at[:, tail, :], 4, above),
            cp(slot_ref.at[head, :], slot_v.at[tail, :], 5, above),
        ]

    def part(h):
        return pl.ds(pl.multiple_of(HALF * h, HALF), HALF)

    def y_copy(dest, h):
        return pltpu.make_async_remote_copy(src_ref=sbuf.at[dest, part(h)], dst_ref=rbuf.at[row, part(h)], send_sem=y_send.at[h, dest],
                                            recv_sem=y_recv.at[h, row], device_id=(wave, dest), device_id_type=MESH)

    def y_local(h):
        return pltpu.make_async_copy(sbuf.at[row, part(h)], rbuf.at[row, part(h)], y_recv.at[h, row])

    def y_arrival(src, h):
        return pltpu.make_async_remote_copy(src_ref=sbuf.at[src, part(h)], dst_ref=rbuf.at[src, part(h)], send_sem=y_send.at[h, src],
                                            recv_sem=y_recv.at[h, src], device_id=(wave, src), device_id_type=MESH)

    for t in range(2):
        make_table(t)
    for t in range(2):
        j = first if t == 0 else 1 - first

        def block(h, carry):
            if t == 0:
                def arrived(c, carry):
                    fetch(h, c).wait()
                    return carry

                lax.fori_loop(0, 32, arrived, 0)
            field = jnp.concatenate([xv.at[h, c].reshape(2 * HALF, 128)[...] for c in range(32)], axis=1)
            y = jnp.dot(field, tabs[t][...], preferred_element_type=F32)
            for i in range(4):
                acc[i] = y[:, 128 * i:128 * i + 128]
            if t == 0:
                @pl.when(h == 0)
                def _():
                    pl.semaphore_wait(barrier, 36)

            def message(n, carry):
                i = lax.rem(n + row, 4)
                p = acc[i, pl.ds(0, HALF, stride=2), :]
                r = pltpu.roll(acc[i, pl.ds(1, HALF, stride=2), :], 64, 1)
                direct = 2 * i + j
                mirror = ROWS - 1 - direct
                sbuf[direct, part(h), :] = (r + sgn * p).astype(BF16)
                sbuf[mirror, part(h), :] = (p - sgn * r).astype(BF16)
                for dest in (direct, mirror):
                    @pl.when(dest != row)
                    def _():
                        y_copy(dest, h).start()

                    @pl.when(dest == row)
                    def _():
                        y_local(h).start()
                return carry

            lax.fori_loop(0, 4, message, 0)
            return carry

        lax.fori_loop(0, 2, block, 0)
        if t == 0:
            for copy in edge_copies():
                copy.start()

    zacc[...] = jnp.zeros_like(zacc)
    mine = lax.rem(jnp.where(row < ROWS // 2, row, ROWS - 1 - row), 2)

    def source(i):
        y = lax.rem(row // 4 + lax.rem(i, 8) // 2, 4)
        return 4 * y + 2 * lax.rem(i, 2) + lax.rem(mine + y + i // 8, 2)

    def absorb(t, carry):
        srcs = [source(2 * t + i) for i in range(2)]
        for src in srcs:
            for h in range(2):
                @pl.when(src == row)
                def _():
                    y_local(h).wait()

                @pl.when(src != row)
                def _():
                    y_arrival(src, h).wait_recv()

        for k in range(2):
            total = None
            for src in srcs:
                rows = pl.ds(pl.multiple_of(src * PR, PR), PR)
                z = lax.dot_general(rbuf[src], tabs[k][rows, :], (((0,), (0,)), ((), ())), preferred_element_type=F32)
                total = z if total is None else total + z
            zacc[k] += total
        return carry

    lax.fori_loop(0, ROWS // 2, absorb, 0)

    flip = row >= ROWS // 2
    last_rows = pl.ds(pl.multiple_of(jnp.where(flip, 0, QR - EXTI), EXTI), EXTI)
    first_rows = pl.ds(pl.multiple_of(jnp.where(flip, QR - EXTI, 0), EXTI), EXTI)
    main = pl.ds(EXTI, QR)
    headi = pl.ds(0, EXTI)
    taili = pl.ds(EXTI + QR, EXTI)

    def i_copy(dest):
        return pltpu.make_async_remote_copy(src_ref=ibuf.at[dest], dst_ref=light_ref.at[wave, main, :], send_sem=i_send.at[dest],
                                            recv_sem=i_recv.at[wave], device_id=(dest, row), device_id_type=MESH)

    def top_copy(dest):
        return pltpu.make_async_remote_copy(src_ref=ibuf.at[dest, last_rows, :], dst_ref=light_ref.at[wave, headi, :], send_sem=e_send.at[0, dest],
                                            recv_sem=e_recv.at[0, wave], device_id=(dest, below), device_id_type=MESH)

    def bot_copy(dest):
        return pltpu.make_async_remote_copy(src_ref=ibuf.at[dest, first_rows, :], dst_ref=light_ref.at[wave, taili, :], send_sem=e_send.at[1, dest],
                                            recv_sem=e_recv.at[1, wave], device_id=(dest, above), device_id_type=MESH)

    def own():
        return pltpu.make_async_copy(ibuf.at[wave], light_ref.at[wave, main, :], i_recv.at[wave])

    sgz = lane_sign((QR, 128))
    low = lax.broadcasted_iota(I32, (QR, 128), 1) < 64

    def intensities(m, carry):
        cols = pl.ds(pl.multiple_of(128 * m, 128), 128)
        direct, mirror = [], []
        for blk in range(2):
            k = jnp.where(first == blk, 0, 1)
            p = zacc[k, 0:QR, cols]
            r = pltpu.roll(zacc[k, QR:2 * QR, cols], 64, 1)
            z1 = r + sgz * p
            z2 = p - sgz * r
            z1 = z1 * z1
            z2 = z2 * z2
            direct.append(z1 + pltpu.roll(z1, 64, 1))
            mirror.append(z2 + pltpu.roll(z2, 64, 1))
        ibuf[m] = jnp.where(low, direct[0], direct[1]).astype(BF16)
        ibuf[WAVES - 1 - m] = jnp.where(low, mirror[0], mirror[1]).astype(BF16)
        for dest in (m, WAVES - 1 - m):
            @pl.when(dest != wave)
            def _():
                i_copy(dest).start()

            @pl.when(dest == wave)
            def _():
                own().start()
            top_copy(dest).start()
            bot_copy(dest).start()
        return carry

    lax.fori_loop(0, 4, intensities, 0)

    for copy in locals_:
        copy.wait()
    for copy in edge_copies():
        copy.wait()
    order = lane_order(wave)
    q = lax.broadcasted_iota(I32, (QE, UB), 0)
    base = 4 * (row * QR + q - EXT) - 8 - 4 * (q % 2)

    def prepare(w, carry):
        begin = jnp.clip(start_v[w] - base, -64, 64).astype(F32).astype(BF16)
        begin = jnp.dot(begin, order, preferred_element_type=F32)
        length = jnp.dot(length_v[w].astype(F32).astype(BF16), order, preferred_element_type=F32)
        begin_v[w] = begin.astype(I32)
        count_v[w] = length.astype(I32)
        gain_v[w] = 1.0 / length
        return carry

    lax.fori_loop(0, WAVES, prepare, 0)
    slots_ref[...] = jnp.dot(slot_v[...].astype(F32).astype(BF16), order, preferred_element_type=F32).astype(I32)
    n = lax.broadcasted_iota(I32, (4 * UB, 4 * UB), 0)
    x = lax.broadcasted_iota(I32, (4 * UB, 4 * UB), 1)
    lane = n % UB
    lane = jnp.where(wave >= WAVES // 2, UB - 1 - lane, lane)
    spread_ref[...] = (4 * lane + n // UB == x).astype(F32).astype(BF16)
    sub = lax.broadcasted_iota(I32, (8, UB), 0)

    def make_masks(j, carry):
        for odd in range(2):
            q = 2 * (j + 1) + odd
            for w in range(WAVES):
                f = jnp.broadcast_to(begin_v[w, pl.ds(q, 1), :], (8, UB))
                e = jnp.broadcast_to(count_v[w, pl.ds(q, 1), :], (8, UB)).astype(jnp.uint32)
                g = jnp.broadcast_to(gain_v[w, pl.ds(q, 1), :], (8, UB))
                for k, i in enumerate(window(w, odd)):
                    mask[w, j, odd, 8 * k:8 * k + 8, :] = jnp.where((sub + 8 * i - f).astype(jnp.uint32) < e, g, 0.0)
        return carry

    lax.fori_loop(0, PAIRS, make_masks, 0)
    image[...] = jnp.zeros_like(image)

    def drain(t, carry):
        for h in range(2):
            y_copy(lax.rem(row + t, ROWS), h).wait_send()
        return carry

    lax.fori_loop(1, ROWS, drain, 0)

    def i_arrival(src):
        return pltpu.make_async_remote_copy(src_ref=ibuf.at[src], dst_ref=light_ref.at[src, main, :], send_sem=i_send.at[src],
                                            recv_sem=i_recv.at[src], device_id=(src, row), device_id_type=MESH)

    def top_arrival(src):
        return pltpu.make_async_remote_copy(src_ref=ibuf.at[src, last_rows, :], dst_ref=light_ref.at[src, headi, :], send_sem=e_send.at[0, src],
                                            recv_sem=e_recv.at[0, src], device_id=(src, below), device_id_type=MESH)

    def bot_arrival(src):
        return pltpu.make_async_remote_copy(src_ref=ibuf.at[src, first_rows, :], dst_ref=light_ref.at[src, taili, :], send_sem=e_send.at[1, src],
                                            recv_sem=e_recv.at[1, src], device_id=(src, above), device_id_type=MESH)

    def finish(t, carry):
        src = lax.rem(wave + t, WAVES)

        @pl.when(t != 0)
        def _():
            i_arrival(src).wait()

        @pl.when(t == 0)
        def _():
            own().wait()
        return carry

    def finish_edges(src, carry):
        top_arrival(src).wait()
        bot_arrival(src).wait()
        return carry

    lax.fori_loop(0, WAVES, finish, 0)
    flip_above = above >= ROWS // 2
    flip_below = below >= ROWS // 2
    def held(q):
        n = q - EXT
        top = jnp.where(flip_above, 7 - q, 8 + q)
        mid_at = EXTI + jnp.where(flip, QR - 1 - n, n)
        n = q - EXT - QR
        bot = EXTI + QR + jnp.where(flip_below, EXTI - 1 - n, n)
        return jnp.where(q < EXT, top, jnp.where(q < EXT + QR, mid_at, bot))

    def deposit(j, light):
        light = [list(groups) for groups in light]
        for odd in range(2):
            q = 2 * (j + 1) + odd
            at = held(q)
            strip = [None] * 5
            for w in range(WAVES):
                v = jnp.broadcast_to(lf[w, pl.ds(at, 1), :], (8, UB))
                for k, i in enumerate(window(w, odd)):
                    add = mask[w, j, odd, 8 * k:8 * k + 8, :] * v
                    strip[i] = add if strip[i] is None else strip[i] + add
            c = jnp.broadcast_to(slots_ref[pl.ds(q, 1), :], (8, UB))
            for k in range(4):
                hot = c == k
                for i in range(5):
                    if strip[i] is not None:
                        add = jnp.where(hot, strip[i], 0.0)
                        light[k][i] = add if light[k][i] is None else light[k][i] + add
        return light

    def group(j):
        return pl.ds(pl.multiple_of(8 * j, 8), 8)

    def pair(j, carry):
        light = deposit(j, [list(carry[4 * k:4 * k + 4]) + [None] for k in range(4)])
        for k in range(4):
            image[group(j), UB * k:UB * k + UB] = light[k][0]
        return tuple(light[k][i] for k in range(4) for i in range(1, 5))

    def edge_pair(n, carry):
        j = jnp.where(n < 3, n, PAIRS - 1)
        light = deposit(j, [[None] * 5 for _ in range(4)])
        for k in range(4):
            for i in range(5):
                image[group(j + i), UB * k:UB * k + UB] += light[k][i]
        return carry

    lf[:, EXTI:EXTI + QR, :] = light_ref[:, EXTI:EXTI + QR, :].astype(F32)
    zero = jnp.zeros((8, UB), F32)
    carry = lax.fori_loop(3, PAIRS - 1, pair, (zero,) * 16, unroll=2)
    for k in range(4):
        for i in range(4):
            image[8 * (PAIRS - 1 + i):8 * (PAIRS + i), UB * k:UB * k + UB] = carry[4 * k + i]
    lax.fori_loop(0, WAVES, finish_edges, 0)
    lf[:, 0:EXTI, :] = light_ref[:, 0:EXTI, :].astype(F32)
    lf[:, EXTI + QR:, :] = light_ref[:, EXTI + QR:, :].astype(F32)
    lax.fori_loop(0, 4, edge_pair, 0)
    whole = image[32:32 + 4 * QR, :]
    hi = whole.astype(BF16)
    lo = (whole - hi.astype(F32)).astype(BF16)
    spread = spread_ref[...]
    out_ref[...] = jnp.dot(hi, spread, preferred_element_type=F32) + jnp.dot(lo, spread, preferred_element_type=F32)


def per_device(lyot_field, wave_scale, trace_start, trace_length, column_slot):
    x = lyot_field.reshape(PR, 2, NP // 128, 128).transpose(0, 2, 1, 3)
    vm = pl.BlockSpec(memory_space=pltpu.VMEM)
    hbm = pl.BlockSpec(memory_space=pltpu.HBM)
    dma = pltpu.SemaphoreType.DMA
    return pl.pallas_call(
        k1,
        out_shape=jax.ShapeDtypeStruct((4 * QR, 4 * UB), F32),
        in_specs=[pl.BlockSpec(memory_space=pltpu.SMEM), hbm, hbm, hbm, hbm],
        out_specs=vm,
        scratch_shapes=[
            pltpu.VMEM((WAVES, QR + 2 * EXTI, UB), BF16), pltpu.VMEM((QE, UB), I32), pltpu.VMEM((4 * UB, 4 * UB), BF16),
            pltpu.VMEM((WAVES, PAIRS, 2, 32, UB), F32), pltpu.VMEM((WAVES, QR + 2 * EXTI, UB), F32), pltpu.VMEM((ACC_ROWS, 4 * UB), F32),
            pltpu.VMEM((2, NP // 128, HALF, 2, 128), BF16),
            pltpu.VMEM((128, 512), F32), pltpu.VMEM((128, 512), F32), pltpu.VMEM((32, 512), F32), pltpu.VMEM((32, 512), F32),
            pltpu.VMEM((NP, 512), BF16), pltpu.VMEM((NP, 512), BF16), pltpu.VMEM((4, 2 * HALF, 128), F32),
            pltpu.VMEM((ROWS, PR, 128), BF16), pltpu.VMEM((ROWS, PR, 128), BF16),
            pltpu.VMEM((2, 2 * QR, 512), F32), pltpu.VMEM((WAVES, QR, UB), BF16),
            pltpu.VMEM((WAVES, QE, UB), I32), pltpu.VMEM((WAVES, QE, UB), I32), pltpu.VMEM((QE, UB), I32),
            pltpu.VMEM((WAVES, QE, UB), I32), pltpu.VMEM((WAVES, QE, UB), I32), pltpu.VMEM((WAVES, QE, UB), F32),
            dma((2, NP // 128)), dma((3,)), dma((2, ROWS)), dma((2, ROWS)), dma((WAVES,)), dma((WAVES,)),
            dma((2, WAVES)), dma((2, WAVES)), dma((6,)), dma((6,)),
        ],
        compiler_params=pltpu.CompilerParams(collective_id=0, has_side_effects=True, vmem_limit_bytes=50 << 20),
    )(wave_scale, *[pltpu.with_memory_space_constraint(v, pltpu.HBM) for v in (x, trace_start, trace_length, column_slot)])


def solution(mesh):
    placed = (
        P("wave", "row", None, None),
        P("wave"),
        P(None, "row", "wave"),
        P(None, "row", "wave"),
        P("row", "wave"),
    )
    return jax.shard_map(
        per_device, mesh=mesh, in_specs=placed, out_specs=P("row", "wave"), check_vma=False
    )
```

```python
import jax
import jax.numpy as jnp
from jax import lax
from jax.experimental import pallas as pl
from jax.experimental.pallas import tpu as pltpu
from jax.sharding import PartitionSpec as P

F32, BF16, I32 = jnp.float32, jnp.bfloat16, jnp.int32
MESH = pl.DeviceIdType.MESH
NP = 4096
NQ = 1024
ROWS = 16
WAVES = 8
PR = NP // ROWS
QR = NQ // ROWS
UB = NQ // WAVES
EXT = 8
EXTI = 16
HALF = PR // 2
QE = QR + 2 * EXT
PAIRS = 36
ACC_ROWS = 8 * PAIRS + 40


def sincos_turns(turns):
    frac = turns - jnp.round(turns)
    quad = jnp.round(frac * 4.0)
    r = (frac - quad * 0.25) * 6.283185307179586
    r2 = r * r
    s = r * (1.0 + r2 * (-1.6666667e-1 + r2 * (8.3333310e-3 + r2 * (-1.9840874e-4 + r2 * 2.7525562e-6))))
    c = 1.0 + r2 * (-0.5 + r2 * (4.16666642e-2 + r2 * (-1.3888397e-3 + r2 * 2.4760495e-5)))
    odd = jnp.abs(quad) == 1.0
    cc = jnp.where(odd, s, c)
    ss = jnp.where(odd, c, s)
    cneg = (quad == 1.0) | (jnp.abs(quad) == 2.0)
    sneg = (quad == -1.0) | (jnp.abs(quad) == 2.0)
    return jnp.where(cneg, -cc, cc), jnp.where(sneg, -ss, ss)


def lens_lanes(shape, half):
    n = lax.broadcasted_iota(I32, shape, 1)
    i = n % 128
    k = 64 * (n // 128 + 4 * half) + i % 64
    return k.astype(F32) - 511.5, i >= 64


def lane_sign(shape):
    return jnp.where(lax.broadcasted_iota(I32, shape, 1) < 64, 1.0, -1.0).astype(F32)


def lane_order(wave):
    n = lax.broadcasted_iota(I32, (UB, UB), 0)
    x = lax.broadcasted_iota(I32, (UB, UB), 1)
    return (n == jnp.where(wave >= WAVES // 2, UB - 1 - x, x)).astype(F32).astype(BF16)


def window(w, odd):
    return range((w + 4 * odd) // 8, (w + 4 * odd + 22) // 8 + 1)


def k1(scale_ref, x_ref, start_ref, length_ref, slot_ref,
       out_ref,
       light_ref, slots_ref, spread_ref, mask, lf, image,
       xv, lo_u, lo_v, hi_c, hi_s, tab0, tab1, acc, sbuf, rbuf, zacc, ibuf, start_v, length_v, slot_v, begin_v, count_v, gain_v,
       x_sem, own_sem, y_send, y_recv, i_send, i_recv, e_send, e_recv, t_send, t_recv):
    wave = lax.axis_index("wave")
    row = lax.axis_index("row")
    below = lax.rem(row + 1, ROWS)
    above = lax.rem(row + ROWS - 1, ROWS)
    tabs = (tab0, tab1)

    def fetch(h, c):
        return pltpu.make_async_copy(x_ref.at[pl.ds(HALF * h, HALF), c], xv.at[h, c], x_sem.at[h, c])

    for c in range(32):
        fetch(0, c).start()

    barrier = pltpu.get_barrier_semaphore()

    def greet_row(i, carry):
        pl.semaphore_signal(barrier, inc=1, device_id=(wave, lax.rem(row + i, ROWS)), device_id_type=MESH)
        return carry

    def greet_wave(i, carry):
        pl.semaphore_signal(barrier, inc=1, device_id=(lax.rem(wave + i, WAVES), row), device_id_type=MESH)
        pl.semaphore_signal(barrier, inc=1, device_id=(lax.rem(wave + i, WAVES), below), device_id_type=MESH)
        pl.semaphore_signal(barrier, inc=1, device_id=(lax.rem(wave + i, WAVES), above), device_id_type=MESH)
        return carry

    lax.fori_loop(1, ROWS, greet_row, 0)
    lax.fori_loop(1, WAVES, greet_wave, 0)

    mid = slice(EXT, EXT + QR)
    locals_ = [
        pltpu.make_async_copy(start_ref, start_v.at[:, mid, :], own_sem.at[0]),
        pltpu.make_async_copy(length_ref, length_v.at[:, mid, :], own_sem.at[1]),
        pltpu.make_async_copy(slot_ref, slot_v.at[mid, :], own_sem.at[2]),
    ]
    for copy in locals_:
        copy.start()

    first = lax.rem(row, 2)
    s = scale_ref[0] * (1.0 / NP)

    def make_table(t):
        j = first if t == 0 else 1 - first
        y, is_sin = lens_lanes((128, 512), j)
        b = lax.broadcasted_iota(I32, (128, 512), 0).astype(F32) - 63.5
        c, sn = sincos_turns(b * y * s)
        lo_u[...] = jnp.where(is_sin, sn, c) * (1.0 / 64.0)
        lo_v[...] = jnp.where(is_sin, c, -sn) * (1.0 / 64.0)
        y, is_sin = lens_lanes((32, 512), j)
        a = lax.broadcasted_iota(I32, (32, 512), 0).astype(F32) * 128.0 - 1984.0
        c, sn = sincos_turns(a * y * s)
        hi_c[...] = c
        hi_s[...] = sn

        def make(a, carry):
            rows = pl.ds(pl.multiple_of(a * 128, 128), 128)
            tabs[t][rows, :] = (lo_u[...] * hi_c[pl.ds(a, 1), :] + lo_v[...] * hi_s[pl.ds(a, 1), :]).astype(BF16)
            return carry

        lax.fori_loop(0, 32, make, 0)

    sgn = lane_sign((HALF, 128))

    def edge_copies():
        def cp(src, dst, i, dev):
            return pltpu.make_async_remote_copy(src_ref=src, dst_ref=dst, send_sem=t_send.at[i], recv_sem=t_recv.at[i],
                                                device_id=(wave, dev), device_id_type=MESH)
        last = slice(QR - EXT, QR)
        head = slice(0, EXT)
        tail = slice(EXT + QR, QR + 2 * EXT)
        return [
            cp(start_ref.at[:, last, :], start_v.at[:, head, :], 0, below),
            cp(length_ref.at[:, last, :], length_v.at[:, head, :], 1, below),
            cp(slot_ref.at[last, :], slot_v.at[head, :], 2, below),
            cp(start_ref.at[:, head, :], start_v.at[:, tail, :], 3, above),
            cp(length_ref.at[:, head, :], length_v.at[:, tail, :], 4, above),
            cp(slot_ref.at[head, :], slot_v.at[tail, :], 5, above),
        ]

    def part(h):
        return pl.ds(pl.multiple_of(HALF * h, HALF), HALF)

    def y_copy(dest, h):
        return pltpu.make_async_remote_copy(src_ref=sbuf.at[dest, part(h)], dst_ref=rbuf.at[row, part(h)], send_sem=y_send.at[h, dest],
                                            recv_sem=y_recv.at[h, row], device_id=(wave, dest), device_id_type=MESH)

    def y_local(h):
        return pltpu.make_async_copy(sbuf.at[row, part(h)], rbuf.at[row, part(h)], y_recv.at[h, row])

    def y_arrival(src, h):
        return pltpu.make_async_remote_copy(src_ref=sbuf.at[src, part(h)], dst_ref=rbuf.at[src, part(h)], send_sem=y_send.at[h, src],
                                            recv_sem=y_recv.at[h, src], device_id=(wave, src), device_id_type=MESH)

    for t in range(2):
        make_table(t)
    for c in range(32):
        fetch(1, c).start()
    for t in range(2):
        j = first if t == 0 else 1 - first

        def block(h, carry):
            if t == 0:
                def arrived(c, carry):
                    fetch(h, c).wait()
                    return carry

                lax.fori_loop(0, 32, arrived, 0)
            field = jnp.concatenate([xv.at[h, c].reshape(2 * HALF, 128)[...] for c in range(32)], axis=1)
            y = jnp.dot(field, tabs[t][...], preferred_element_type=F32)
            for i in range(4):
                acc[i] = y[:, 128 * i:128 * i + 128]
            if t == 0:
                @pl.when(h == 0)
                def _():
                    pl.semaphore_wait(barrier, 36)

            def message(n, carry):
                i = lax.rem(n + row, 4)
                p = acc[i, pl.ds(0, HALF, stride=2), :]
                r = pltpu.roll(acc[i, pl.ds(1, HALF, stride=2), :], 64, 1)
                direct = 4 * j + i
                mirror = ROWS - 1 - direct
                sbuf[direct, part(h), :] = (r + sgn * p).astype(BF16)
                sbuf[mirror, part(h), :] = (p - sgn * r).astype(BF16)
                for dest in (direct, mirror):
                    @pl.when(dest != row)
                    def _():
                        y_copy(dest, h).start()

                    @pl.when(dest == row)
                    def _():
                        y_local(h).start()
                return carry

            lax.fori_loop(0, 4, message, 0)
            return carry

        lax.fori_loop(0, 2, block, 0)
        if t == 0:
            for copy in edge_copies():
                copy.start()

    zacc[...] = jnp.zeros_like(zacc)
    band = row // 4
    early = jnp.where((band == 0) | (band == 3), 0, 1)

    def source(i):
        return 2 * lax.rem(row // 2 + i, 8) + jnp.where(i < 8, early, 1 - early)

    def absorb(t, carry):
        srcs = [source(2 * t + i) for i in range(2)]
        for src in srcs:
            for h in range(2):
                @pl.when(src == row)
                def _():
                    y_local(h).wait()

                @pl.when(src != row)
                def _():
                    y_arrival(src, h).wait_recv()

        for k in range(2):
            total = None
            for src in srcs:
                rows = pl.ds(pl.multiple_of(src * PR, PR), PR)
                z = lax.dot_general(rbuf[src], tabs[k][rows, :], (((0,), (0,)), ((), ())), preferred_element_type=F32)
                total = z if total is None else total + z
            zacc[k] += total
        return carry

    lax.fori_loop(0, ROWS // 2, absorb, 0)

    flip = row >= ROWS // 2
    last_rows = pl.ds(pl.multiple_of(jnp.where(flip, 0, QR - EXTI), EXTI), EXTI)
    first_rows = pl.ds(pl.multiple_of(jnp.where(flip, QR - EXTI, 0), EXTI), EXTI)
    main = pl.ds(EXTI, QR)
    headi = pl.ds(0, EXTI)
    taili = pl.ds(EXTI + QR, EXTI)

    def i_copy(dest):
        return pltpu.make_async_remote_copy(src_ref=ibuf.at[dest], dst_ref=light_ref.at[wave, main, :], send_sem=i_send.at[dest],
                                            recv_sem=i_recv.at[wave], device_id=(dest, row), device_id_type=MESH)

    def top_copy(dest):
        return pltpu.make_async_remote_copy(src_ref=ibuf.at[dest, last_rows, :], dst_ref=light_ref.at[wave, headi, :], send_sem=e_send.at[0, dest],
                                            recv_sem=e_recv.at[0, wave], device_id=(dest, below), device_id_type=MESH)

    def bot_copy(dest):
        return pltpu.make_async_remote_copy(src_ref=ibuf.at[dest, first_rows, :], dst_ref=light_ref.at[wave, taili, :], send_sem=e_send.at[1, dest],
                                            recv_sem=e_recv.at[1, wave], device_id=(dest, above), device_id_type=MESH)

    def own():
        return pltpu.make_async_copy(ibuf.at[wave], light_ref.at[wave, main, :], i_recv.at[wave])

    sgz = lane_sign((QR, 128))
    low = lax.broadcasted_iota(I32, (QR, 128), 1) < 64

    def intensities(m, carry):
        k = jnp.where(first == m // 2, 0, 1)
        direct, mirror = [], []
        for blk in range(2):
            cols = pl.ds(pl.multiple_of(256 * lax.rem(m, 2) + 128 * blk, 128), 128)
            p = zacc[k, 0:QR, cols]
            r = pltpu.roll(zacc[k, QR:2 * QR, cols], 64, 1)
            z1 = r + sgz * p
            z2 = p - sgz * r
            z1 = z1 * z1
            z2 = z2 * z2
            direct.append(z1 + pltpu.roll(z1, 64, 1))
            mirror.append(z2 + pltpu.roll(z2, 64, 1))
        ibuf[m] = jnp.where(low, direct[0], direct[1]).astype(BF16)
        ibuf[WAVES - 1 - m] = jnp.where(low, mirror[0], mirror[1]).astype(BF16)
        for dest in (m, WAVES - 1 - m):
            @pl.when(dest != wave)
            def _():
                i_copy(dest).start()

            @pl.when(dest == wave)
            def _():
                own().start()
            top_copy(dest).start()
            bot_copy(dest).start()
        return carry

    lax.fori_loop(0, 4, intensities, 0)

    for copy in locals_:
        copy.wait()
    for copy in edge_copies():
        copy.wait()
    order = lane_order(wave)
    q = lax.broadcasted_iota(I32, (QE, UB), 0)
    base = 4 * (row * QR + q - EXT) - 8 - 4 * (q % 2)

    def prepare(w, carry):
        begin = jnp.clip(start_v[w] - base, -64, 64).astype(F32).astype(BF16)
        begin = jnp.dot(begin, order, preferred_element_type=F32)
        length = jnp.dot(length_v[w].astype(F32).astype(BF16), order, preferred_element_type=F32)
        begin_v[w] = begin.astype(I32)
        count_v[w] = length.astype(I32)
        gain_v[w] = 1.0 / length
        return carry

    lax.fori_loop(0, WAVES, prepare, 0)
    slots_ref[...] = jnp.dot(slot_v[...].astype(F32).astype(BF16), order, preferred_element_type=F32).astype(I32)
    n = lax.broadcasted_iota(I32, (4 * UB, 4 * UB), 0)
    x = lax.broadcasted_iota(I32, (4 * UB, 4 * UB), 1)
    lane = n % UB
    lane = jnp.where(wave >= WAVES // 2, UB - 1 - lane, lane)
    spread_ref[...] = (4 * lane + n // UB == x).astype(F32).astype(BF16)
    sub = lax.broadcasted_iota(I32, (8, UB), 0)

    def make_masks(j, carry):
        for odd in range(2):
            q = 2 * (j + 1) + odd
            for w in range(WAVES):
                f = jnp.broadcast_to(begin_v[w, pl.ds(q, 1), :], (8, UB))
                e = jnp.broadcast_to(count_v[w, pl.ds(q, 1), :], (8, UB)).astype(jnp.uint32)
                g = jnp.broadcast_to(gain_v[w, pl.ds(q, 1), :], (8, UB))
                for k, i in enumerate(window(w, odd)):
                    mask[w, j, odd, 8 * k:8 * k + 8, :] = jnp.where((sub + 8 * i - f).astype(jnp.uint32) < e, g, 0.0)
        return carry

    lax.fori_loop(0, PAIRS, make_masks, 0)
    image[...] = jnp.zeros_like(image)

    def drain(t, carry):
        for h in range(2):
            y_copy(lax.rem(row + t, ROWS), h).wait_send()
        return carry

    lax.fori_loop(1, ROWS, drain, 0)

    def i_arrival(src):
        return pltpu.make_async_remote_copy(src_ref=ibuf.at[src], dst_ref=light_ref.at[src, main, :], send_sem=i_send.at[src],
                                            recv_sem=i_recv.at[src], device_id=(src, row), device_id_type=MESH)

    def top_arrival(src):
        return pltpu.make_async_remote_copy(src_ref=ibuf.at[src, last_rows, :], dst_ref=light_ref.at[src, headi, :], send_sem=e_send.at[0, src],
                                            recv_sem=e_recv.at[0, src], device_id=(src, below), device_id_type=MESH)

    def bot_arrival(src):
        return pltpu.make_async_remote_copy(src_ref=ibuf.at[src, first_rows, :], dst_ref=light_ref.at[src, taili, :], send_sem=e_send.at[1, src],
                                            recv_sem=e_recv.at[1, src], device_id=(src, above), device_id_type=MESH)

    def finish(t, carry):
        src = lax.rem(wave + t, WAVES)

        @pl.when(t != 0)
        def _():
            i_arrival(src).wait()

        @pl.when(t == 0)
        def _():
            own().wait()
        return carry

    def finish_edges(src, carry):
        top_arrival(src).wait()
        bot_arrival(src).wait()
        return carry

    lax.fori_loop(0, WAVES, finish, 0)
    flip_above = above >= ROWS // 2
    flip_below = below >= ROWS // 2
    def held(q):
        n = q - EXT
        top = jnp.where(flip_above, 7 - q, 8 + q)
        mid_at = EXTI + jnp.where(flip, QR - 1 - n, n)
        n = q - EXT - QR
        bot = EXTI + QR + jnp.where(flip_below, EXTI - 1 - n, n)
        return jnp.where(q < EXT, top, jnp.where(q < EXT + QR, mid_at, bot))

    def deposit(j, light):
        light = [list(groups) for groups in light]
        for odd in range(2):
            q = 2 * (j + 1) + odd
            at = held(q)
            strip = [None] * 5
            for w in range(WAVES):
                v = jnp.broadcast_to(lf[w, pl.ds(at, 1), :], (8, UB))
                for k, i in enumerate(window(w, odd)):
                    add = mask[w, j, odd, 8 * k:8 * k + 8, :] * v
                    strip[i] = add if strip[i] is None else strip[i] + add
            c = jnp.broadcast_to(slots_ref[pl.ds(q, 1), :], (8, UB))
            for k in range(4):
                hot = c == k
                for i in range(5):
                    if strip[i] is not None:
                        add = jnp.where(hot, strip[i], 0.0)
                        light[k][i] = add if light[k][i] is None else light[k][i] + add
        return light

    def group(j):
        return pl.ds(pl.multiple_of(8 * j, 8), 8)

    def pair(j, carry):
        light = deposit(j, [list(carry[4 * k:4 * k + 4]) + [None] for k in range(4)])
        for k in range(4):
            image[group(j), UB * k:UB * k + UB] = light[k][0]
        return tuple(light[k][i] for k in range(4) for i in range(1, 5))

    def edge_pair(n, carry):
        j = jnp.where(n < 3, n, PAIRS - 1)
        light = deposit(j, [[None] * 5 for _ in range(4)])
        for k in range(4):
            for i in range(5):
                image[group(j + i), UB * k:UB * k + UB] += light[k][i]
        return carry

    lf[:, EXTI:EXTI + QR, :] = light_ref[:, EXTI:EXTI + QR, :].astype(F32)
    zero = jnp.zeros((8, UB), F32)
    carry = lax.fori_loop(3, PAIRS - 1, pair, (zero,) * 16, unroll=2)
    for k in range(4):
        for i in range(4):
            image[8 * (PAIRS - 1 + i):8 * (PAIRS + i), UB * k:UB * k + UB] = carry[4 * k + i]
    lax.fori_loop(0, WAVES, finish_edges, 0)
    lf[:, 0:EXTI, :] = light_ref[:, 0:EXTI, :].astype(F32)
    lf[:, EXTI + QR:, :] = light_ref[:, EXTI + QR:, :].astype(F32)
    lax.fori_loop(0, 4, edge_pair, 0)
    whole = image[32:32 + 4 * QR, :]
    hi = whole.astype(BF16)
    lo = (whole - hi.astype(F32)).astype(BF16)
    spread = spread_ref[...]
    out_ref[...] = jnp.dot(hi, spread, preferred_element_type=F32) + jnp.dot(lo, spread, preferred_element_type=F32)


def per_device(lyot_field, wave_scale, trace_start, trace_length, column_slot):
    x = lyot_field.reshape(PR, 2, NP // 128, 128).transpose(0, 2, 1, 3)
    vm = pl.BlockSpec(memory_space=pltpu.VMEM)
    hbm = pl.BlockSpec(memory_space=pltpu.HBM)
    dma = pltpu.SemaphoreType.DMA
    return pl.pallas_call(
        k1,
        out_shape=jax.ShapeDtypeStruct((4 * QR, 4 * UB), F32),
        in_specs=[pl.BlockSpec(memory_space=pltpu.SMEM), hbm, hbm, hbm, hbm],
        out_specs=vm,
        scratch_shapes=[
            pltpu.VMEM((WAVES, QR + 2 * EXTI, UB), BF16), pltpu.VMEM((QE, UB), I32), pltpu.VMEM((4 * UB, 4 * UB), BF16),
            pltpu.VMEM((WAVES, PAIRS, 2, 32, UB), F32), pltpu.VMEM((WAVES, QR + 2 * EXTI, UB), F32), pltpu.VMEM((ACC_ROWS, 4 * UB), F32),
            pltpu.VMEM((2, NP // 128, HALF, 2, 128), BF16),
            pltpu.VMEM((128, 512), F32), pltpu.VMEM((128, 512), F32), pltpu.VMEM((32, 512), F32), pltpu.VMEM((32, 512), F32),
            pltpu.VMEM((NP, 512), BF16), pltpu.VMEM((NP, 512), BF16), pltpu.VMEM((4, 2 * HALF, 128), F32),
            pltpu.VMEM((ROWS, PR, 128), BF16), pltpu.VMEM((ROWS, PR, 128), BF16),
            pltpu.VMEM((2, 2 * QR, 512), F32), pltpu.VMEM((WAVES, QR, UB), BF16),
            pltpu.VMEM((WAVES, QE, UB), I32), pltpu.VMEM((WAVES, QE, UB), I32), pltpu.VMEM((QE, UB), I32),
            pltpu.VMEM((WAVES, QE, UB), I32), pltpu.VMEM((WAVES, QE, UB), I32), pltpu.VMEM((WAVES, QE, UB), F32),
            dma((2, NP // 128)), dma((3,)), dma((2, ROWS)), dma((2, ROWS)), dma((WAVES,)), dma((WAVES,)),
            dma((2, WAVES)), dma((2, WAVES)), dma((6,)), dma((6,)),
        ],
        compiler_params=pltpu.CompilerParams(collective_id=0, has_side_effects=True, vmem_limit_bytes=50 << 20),
    )(wave_scale, *[pltpu.with_memory_space_constraint(v, pltpu.HBM) for v in (x, trace_start, trace_length, column_slot)])


def solution(mesh):
    placed = (
        P("wave", "row", None, None),
        P("wave"),
        P(None, "row", "wave"),
        P(None, "row", "wave"),
        P("row", "wave"),
    )
    return jax.shard_map(
        per_device, mesh=mesh, in_specs=placed, out_specs=P("row", "wave"), check_vma=False
    )
```

```python
import jax
import jax.numpy as jnp
from jax import lax
from jax.experimental import pallas as pl
from jax.experimental.pallas import tpu as pltpu
from jax.sharding import PartitionSpec as P

F32, BF16, I32 = jnp.float32, jnp.bfloat16, jnp.int32
MESH = pl.DeviceIdType.MESH
NP = 4096
NQ = 1024
ROWS = 16
WAVES = 8
PR = NP // ROWS
QR = NQ // ROWS
UB = NQ // WAVES
EXT = 8
EXTI = 16
HALF = PR // 2
QE = QR + 2 * EXT
PAIRS = 36
ACC_ROWS = 8 * PAIRS + 40


def sincos_turns(turns):
    frac = turns - jnp.round(turns)
    quad = jnp.round(frac * 4.0)
    r = (frac - quad * 0.25) * 6.283185307179586
    r2 = r * r
    s = r * (1.0 + r2 * (-1.6666667e-1 + r2 * (8.3333310e-3 + r2 * (-1.9840874e-4 + r2 * 2.7525562e-6))))
    c = 1.0 + r2 * (-0.5 + r2 * (4.16666642e-2 + r2 * (-1.3888397e-3 + r2 * 2.4760495e-5)))
    odd = jnp.abs(quad) == 1.0
    cc = jnp.where(odd, s, c)
    ss = jnp.where(odd, c, s)
    cneg = (quad == 1.0) | (jnp.abs(quad) == 2.0)
    sneg = (quad == -1.0) | (jnp.abs(quad) == 2.0)
    return jnp.where(cneg, -cc, cc), jnp.where(sneg, -ss, ss)


def lane_sign(shape):
    return jnp.where(lax.broadcasted_iota(I32, shape, 1) < 64, 1.0, -1.0).astype(F32)


def lane_order(wave):
    n = lax.broadcasted_iota(I32, (UB, UB), 0)
    x = lax.broadcasted_iota(I32, (UB, UB), 1)
    return (n == jnp.where(wave >= WAVES // 2, UB - 1 - x, x)).astype(F32).astype(BF16)


def window(w, odd):
    return range((w + 4 * odd) // 8, (w + 4 * odd + 22) // 8 + 1)


def k1(scale_ref, x_ref, start_ref, length_ref, slot_ref,
       out_ref,
       light_ref, slots_ref, spread_ref, mask, lf, image,
       xv, lo_u, lo_v, hi_c, hi_s, tab0, tab1, acc, sbuf, rbuf, zacc, ibuf, start_v, length_v, slot_v, begin_v, count_v, gain_v,
       x_sem, own_sem, y_send, y_recv, i_send, i_recv, e_send, e_recv, t_send, t_recv):
    wave = lax.axis_index("wave")
    row = lax.axis_index("row")
    below = lax.rem(row + 1, ROWS)
    above = lax.rem(row + ROWS - 1, ROWS)
    tabs = (tab0, tab1)

    def fetch(h, c):
        return pltpu.make_async_copy(x_ref.at[pl.ds(HALF * h, HALF), c], xv.at[h, c], x_sem.at[h, c])

    for c in range(32):
        fetch(0, c).start()

    barrier = pltpu.get_barrier_semaphore()

    def greet_row(i, carry):
        pl.semaphore_signal(barrier, inc=1, device_id=(wave, lax.rem(row + i, ROWS)), device_id_type=MESH)
        return carry

    def greet_wave(i, carry):
        pl.semaphore_signal(barrier, inc=1, device_id=(lax.rem(wave + i, WAVES), row), device_id_type=MESH)
        pl.semaphore_signal(barrier, inc=1, device_id=(lax.rem(wave + i, WAVES), below), device_id_type=MESH)
        pl.semaphore_signal(barrier, inc=1, device_id=(lax.rem(wave + i, WAVES), above), device_id_type=MESH)
        return carry

    lax.fori_loop(1, ROWS, greet_row, 0)
    lax.fori_loop(1, WAVES, greet_wave, 0)

    mid = slice(EXT, EXT + QR)
    locals_ = [
        pltpu.make_async_copy(start_ref, start_v.at[:, mid, :], own_sem.at[0]),
        pltpu.make_async_copy(length_ref, length_v.at[:, mid, :], own_sem.at[1]),
        pltpu.make_async_copy(slot_ref, slot_v.at[mid, :], own_sem.at[2]),
    ]
    for copy in locals_:
        copy.start()

    first = lax.rem(row + row // 4, 2)
    s = scale_ref[0] * (1.0 / NP)

    def make_table(t):
        j = first if t == 0 else 1 - first
        low = lax.broadcasted_iota(I32, (128, 128), 1) < 64
        for v in range(2):
            n = lax.broadcasted_iota(I32, (1, 128), 1)
            k = 64 * (2 * (2 * v + n // 64) + j) + n % 64
            y = k.astype(F32) - 511.5
            b = lax.broadcasted_iota(I32, (128, 128), 0).astype(F32) - 63.5
            c, sn = sincos_turns(b * y * s)
            c = c * (1.0 / 64.0)
            sn = sn * (1.0 / 64.0)
            cr = pltpu.roll(c, 64, 1)
            sr = pltpu.roll(sn, 64, 1)
            one, two = slice(256 * v, 256 * v + 128), slice(256 * v + 128, 256 * v + 256)
            lo_u[:, one] = jnp.where(low, c, sr)
            lo_u[:, two] = jnp.where(low, cr, sn)
            lo_v[:, one] = jnp.where(low, -sn, cr)
            lo_v[:, two] = jnp.where(low, -sr, c)
            a = lax.broadcasted_iota(I32, (32, 128), 0).astype(F32) * 128.0 - 1984.0
            c, sn = sincos_turns(a * y * s)
            cr = pltpu.roll(c, 64, 1)
            sr = pltpu.roll(sn, 64, 1)
            hi_c[:, one] = jnp.where(low[0:32], c, cr)
            hi_c[:, two] = jnp.where(low[0:32], cr, c)
            hi_s[:, one] = jnp.where(low[0:32], sn, sr)
            hi_s[:, two] = jnp.where(low[0:32], sr, sn)

        def make(a, carry):
            rows = pl.ds(pl.multiple_of(a * 128, 128), 128)
            tabs[t][rows, :] = (lo_u[...] * hi_c[pl.ds(a, 1), :] + lo_v[...] * hi_s[pl.ds(a, 1), :]).astype(BF16)
            return carry

        lax.fori_loop(0, 32, make, 0)

    sgn = lane_sign((HALF, 128))

    def edge_copies():
        def cp(src, dst, i, dev):
            return pltpu.make_async_remote_copy(src_ref=src, dst_ref=dst, send_sem=t_send.at[i], recv_sem=t_recv.at[i],
                                                device_id=(wave, dev), device_id_type=MESH)
        last = slice(QR - EXT, QR)
        head = slice(0, EXT)
        tail = slice(EXT + QR, QR + 2 * EXT)
        return [
            cp(start_ref.at[:, last, :], start_v.at[:, head, :], 0, below),
            cp(length_ref.at[:, last, :], length_v.at[:, head, :], 1, below),
            cp(slot_ref.at[last, :], slot_v.at[head, :], 2, below),
            cp(start_ref.at[:, head, :], start_v.at[:, tail, :], 3, above),
            cp(length_ref.at[:, head, :], length_v.at[:, tail, :], 4, above),
            cp(slot_ref.at[head, :], slot_v.at[tail, :], 5, above),
        ]

    def part(h):
        return pl.ds(pl.multiple_of(HALF * h, HALF), HALF)

    def y_copy(dest, h):
        return pltpu.make_async_remote_copy(src_ref=sbuf.at[dest, part(h)], dst_ref=rbuf.at[row, part(h)], send_sem=y_send.at[h, dest],
                                            recv_sem=y_recv.at[h, row], device_id=(wave, dest), device_id_type=MESH)

    def y_local(h):
        return pltpu.make_async_copy(sbuf.at[row, part(h)], rbuf.at[row, part(h)], y_recv.at[h, row])

    def y_arrival(src, h):
        return pltpu.make_async_remote_copy(src_ref=sbuf.at[src, part(h)], dst_ref=rbuf.at[src, part(h)], send_sem=y_send.at[h, src],
                                            recv_sem=y_recv.at[h, src], device_id=(wave, src), device_id_type=MESH)

    for t in range(2):
        make_table(t)
        if t == 0:
            for c in range(32):
                fetch(1, c).start()
        j = first if t == 0 else 1 - first

        def block(h, carry):
            if t == 0:
                def arrived(c, carry):
                    fetch(h, c).wait()
                    return carry

                lax.fori_loop(0, 32, arrived, 0)
            field = jnp.concatenate([xv.at[h, c].reshape(2 * HALF, 128)[...] for c in range(32)], axis=1)
            y = jnp.dot(field, tabs[t][...], preferred_element_type=F32)
            for i in range(4):
                acc[i] = y[:, 128 * i:128 * i + 128]
            if t == 0:
                @pl.when(h == 0)
                def _():
                    pl.semaphore_wait(barrier, 36)

            def message(n, carry):
                i = lax.rem(n + row, 4)
                p = acc[i, pl.ds(0, HALF, stride=2), :]
                r = pltpu.roll(acc[i, pl.ds(1, HALF, stride=2), :], 64, 1)
                direct = 2 * i + j
                mirror = ROWS - 1 - direct
                sbuf[direct, part(h), :] = (r + sgn * p).astype(BF16)
                sbuf[mirror, part(h), :] = (p - sgn * r).astype(BF16)
                for dest in (direct, mirror):
                    @pl.when(dest != row)
                    def _():
                        y_copy(dest, h).start()

                    @pl.when(dest == row)
                    def _():
                        y_local(h).start()
                return carry

            lax.fori_loop(0, 4, message, 0)
            return carry

        lax.fori_loop(0, 2, block, 0)
        if t == 0:
            for copy in edge_copies():
                copy.start()

    zacc[...] = jnp.zeros_like(zacc)
    mine = lax.rem(jnp.where(row < ROWS // 2, row, ROWS - 1 - row), 2)

    def source(i):
        y = lax.rem(row // 4 + lax.rem(i, 8) // 2, 4)
        return 4 * y + 2 * lax.rem(i, 2) + lax.rem(mine + y + i // 8, 2)

    def absorb(t, carry):
        srcs = [source(2 * t + i) for i in range(2)]
        for src in srcs:
            for h in range(2):
                @pl.when(src == row)
                def _():
                    y_local(h).wait()

                @pl.when(src != row)
                def _():
                    y_arrival(src, h).wait_recv()

        for k in range(2):
            total = None
            for src in srcs:
                rows = pl.ds(pl.multiple_of(src * PR, PR), PR)
                z = lax.dot_general(rbuf[src], tabs[k][rows, :], (((0,), (0,)), ((), ())), preferred_element_type=F32)
                total = z if total is None else total + z
            zacc[k] += total
        return carry

    lax.fori_loop(0, ROWS // 2, absorb, 0)

    flip = row >= ROWS // 2
    last_rows = pl.ds(pl.multiple_of(jnp.where(flip, 0, QR - EXTI), EXTI), EXTI)
    first_rows = pl.ds(pl.multiple_of(jnp.where(flip, QR - EXTI, 0), EXTI), EXTI)
    main = pl.ds(EXTI, QR)
    headi = pl.ds(0, EXTI)
    taili = pl.ds(EXTI + QR, EXTI)

    def i_copy(dest):
        return pltpu.make_async_remote_copy(src_ref=ibuf.at[dest], dst_ref=light_ref.at[wave, main, :], send_sem=i_send.at[dest],
                                            recv_sem=i_recv.at[wave], device_id=(dest, row), device_id_type=MESH)

    def top_copy(dest):
        return pltpu.make_async_remote_copy(src_ref=ibuf.at[dest, last_rows, :], dst_ref=light_ref.at[wave, headi, :], send_sem=e_send.at[0, dest],
                                            recv_sem=e_recv.at[0, wave], device_id=(dest, below), device_id_type=MESH)

    def bot_copy(dest):
        return pltpu.make_async_remote_copy(src_ref=ibuf.at[dest, first_rows, :], dst_ref=light_ref.at[wave, taili, :], send_sem=e_send.at[1, dest],
                                            recv_sem=e_recv.at[1, wave], device_id=(dest, above), device_id_type=MESH)

    def own():
        return pltpu.make_async_copy(ibuf.at[wave], light_ref.at[wave, main, :], i_recv.at[wave])

    sgz = lane_sign((QR, 128))
    low = lax.broadcasted_iota(I32, (QR, 128), 1) < 64

    def intensities(m, carry):
        cols = pl.ds(pl.multiple_of(128 * m, 128), 128)
        direct, mirror = [], []
        for blk in range(2):
            k = jnp.where(first == blk, 0, 1)
            p = zacc[k, 0:QR, cols]
            r = pltpu.roll(zacc[k, QR:2 * QR, cols], 64, 1)
            z1 = r + sgz * p
            z2 = p - sgz * r
            z1 = z1 * z1
            z2 = z2 * z2
            direct.append(z1 + pltpu.roll(z1, 64, 1))
            mirror.append(z2 + pltpu.roll(z2, 64, 1))
        ibuf[m] = jnp.where(low, direct[0], direct[1]).astype(BF16)
        ibuf[WAVES - 1 - m] = jnp.where(low, mirror[0], mirror[1]).astype(BF16)
        for dest in (m, WAVES - 1 - m):
            @pl.when(dest != wave)
            def _():
                i_copy(dest).start()

            @pl.when(dest == wave)
            def _():
                own().start()
            top_copy(dest).start()
            bot_copy(dest).start()
        return carry

    lax.fori_loop(0, 4, intensities, 0)

    for copy in locals_:
        copy.wait()
    for copy in edge_copies():
        copy.wait()
    order = lane_order(wave)
    q = lax.broadcasted_iota(I32, (QE, UB), 0)
    base = 4 * (row * QR + q - EXT) - 8 - 4 * (q % 2)

    def prepare(w, carry):
        begin = jnp.clip(start_v[w] - base, -64, 64).astype(F32).astype(BF16)
        begin = jnp.dot(begin, order, preferred_element_type=F32)
        length = jnp.dot(length_v[w].astype(F32).astype(BF16), order, preferred_element_type=F32)
        begin_v[w] = begin.astype(I32)
        count_v[w] = length.astype(I32)
        gain_v[w] = 1.0 / length
        return carry

    lax.fori_loop(0, WAVES, prepare, 0)
    slots_ref[...] = jnp.dot(slot_v[...].astype(F32).astype(BF16), order, preferred_element_type=F32).astype(I32)
    n = lax.broadcasted_iota(I32, (4 * UB, 4 * UB), 0)
    x = lax.broadcasted_iota(I32, (4 * UB, 4 * UB), 1)
    lane = n % UB
    lane = jnp.where(wave >= WAVES // 2, UB - 1 - lane, lane)
    spread_ref[...] = (4 * lane + n // UB == x).astype(F32).astype(BF16)
    sub = lax.broadcasted_iota(I32, (8, UB), 0)

    def make_masks(j, carry):
        for odd in range(2):
            q = 2 * (j + 1) + odd
            for w in range(WAVES):
                f = jnp.broadcast_to(begin_v[w, pl.ds(q, 1), :], (8, UB))
                e = jnp.broadcast_to(count_v[w, pl.ds(q, 1), :], (8, UB)).astype(jnp.uint32)
                g = jnp.broadcast_to(gain_v[w, pl.ds(q, 1), :], (8, UB))
                for k, i in enumerate(window(w, odd)):
                    mask[w, j, odd, 8 * k:8 * k + 8, :] = jnp.where((sub + 8 * i - f).astype(jnp.uint32) < e, g, 0.0)
        return carry

    lax.fori_loop(0, PAIRS, make_masks, 0)
    image[...] = jnp.zeros_like(image)

    def drain(t, carry):
        for h in range(2):
            y_copy(lax.rem(row + t, ROWS), h).wait_send()
        return carry

    lax.fori_loop(1, ROWS, drain, 0)

    def i_arrival(src):
        return pltpu.make_async_remote_copy(src_ref=ibuf.at[src], dst_ref=light_ref.at[src, main, :], send_sem=i_send.at[src],
                                            recv_sem=i_recv.at[src], device_id=(src, row), device_id_type=MESH)

    def top_arrival(src):
        return pltpu.make_async_remote_copy(src_ref=ibuf.at[src, last_rows, :], dst_ref=light_ref.at[src, headi, :], send_sem=e_send.at[0, src],
                                            recv_sem=e_recv.at[0, src], device_id=(src, below), device_id_type=MESH)

    def bot_arrival(src):
        return pltpu.make_async_remote_copy(src_ref=ibuf.at[src, first_rows, :], dst_ref=light_ref.at[src, taili, :], send_sem=e_send.at[1, src],
                                            recv_sem=e_recv.at[1, src], device_id=(src, above), device_id_type=MESH)

    def finish(t, carry):
        src = lax.rem(wave + t, WAVES)

        @pl.when(t != 0)
        def _():
            i_arrival(src).wait()

        @pl.when(t == 0)
        def _():
            own().wait()
        return carry

    def finish_edges(src, carry):
        top_arrival(src).wait()
        bot_arrival(src).wait()
        return carry

    lax.fori_loop(0, WAVES, finish, 0)
    flip_above = above >= ROWS // 2
    flip_below = below >= ROWS // 2
    def held(q):
        n = q - EXT
        top = jnp.where(flip_above, 7 - q, 8 + q)
        mid_at = EXTI + jnp.where(flip, QR - 1 - n, n)
        n = q - EXT - QR
        bot = EXTI + QR + jnp.where(flip_below, EXTI - 1 - n, n)
        return jnp.where(q < EXT, top, jnp.where(q < EXT + QR, mid_at, bot))

    def deposit(j, light):
        light = [list(groups) for groups in light]
        for odd in range(2):
            q = 2 * (j + 1) + odd
            at = held(q)
            strip = [None] * 5
            for w in range(WAVES):
                v = jnp.broadcast_to(lf[w, pl.ds(at, 1), :], (8, UB))
                for k, i in enumerate(window(w, odd)):
                    add = mask[w, j, odd, 8 * k:8 * k + 8, :] * v
                    strip[i] = add if strip[i] is None else strip[i] + add
            c = jnp.broadcast_to(slots_ref[pl.ds(q, 1), :], (8, UB))
            for k in range(4):
                hot = c == k
                for i in range(5):
                    if strip[i] is not None:
                        add = jnp.where(hot, strip[i], 0.0)
                        light[k][i] = add if light[k][i] is None else light[k][i] + add
        return light

    def group(j):
        return pl.ds(pl.multiple_of(8 * j, 8), 8)

    def pair(j, carry):
        light = deposit(j, [list(carry[4 * k:4 * k + 4]) + [None] for k in range(4)])
        for k in range(4):
            image[group(j), UB * k:UB * k + UB] = light[k][0]
        return tuple(light[k][i] for k in range(4) for i in range(1, 5))

    def edge_pair(n, carry):
        j = jnp.where(n < 3, n, PAIRS - 1)
        light = deposit(j, [[None] * 5 for _ in range(4)])
        for k in range(4):
            for i in range(5):
                image[group(j + i), UB * k:UB * k + UB] += light[k][i]
        return carry

    lf[:, EXTI:EXTI + QR, :] = light_ref[:, EXTI:EXTI + QR, :].astype(F32)
    zero = jnp.zeros((8, UB), F32)
    carry = lax.fori_loop(3, PAIRS - 1, pair, (zero,) * 16, unroll=2)
    for k in range(4):
        for i in range(4):
            image[8 * (PAIRS - 1 + i):8 * (PAIRS + i), UB * k:UB * k + UB] = carry[4 * k + i]
    lax.fori_loop(0, WAVES, finish_edges, 0)
    lf[:, 0:EXTI, :] = light_ref[:, 0:EXTI, :].astype(F32)
    lf[:, EXTI + QR:, :] = light_ref[:, EXTI + QR:, :].astype(F32)
    lax.fori_loop(0, 4, edge_pair, 0)
    whole = image[32:32 + 4 * QR, :]
    hi = whole.astype(BF16)
    lo = (whole - hi.astype(F32)).astype(BF16)
    spread = spread_ref[...]
    out_ref[...] = jnp.dot(hi, spread, preferred_element_type=F32) + jnp.dot(lo, spread, preferred_element_type=F32)


def per_device(lyot_field, wave_scale, trace_start, trace_length, column_slot):
    x = lyot_field.reshape(PR, 2, NP // 128, 128).transpose(0, 2, 1, 3)
    vm = pl.BlockSpec(memory_space=pltpu.VMEM)
    hbm = pl.BlockSpec(memory_space=pltpu.HBM)
    dma = pltpu.SemaphoreType.DMA
    return pl.pallas_call(
        k1,
        out_shape=jax.ShapeDtypeStruct((4 * QR, 4 * UB), F32),
        in_specs=[pl.BlockSpec(memory_space=pltpu.SMEM), hbm, hbm, hbm, hbm],
        out_specs=vm,
        scratch_shapes=[
            pltpu.VMEM((WAVES, QR + 2 * EXTI, UB), BF16), pltpu.VMEM((QE, UB), I32), pltpu.VMEM((4 * UB, 4 * UB), BF16),
            pltpu.VMEM((WAVES, PAIRS, 2, 32, UB), F32), pltpu.VMEM((WAVES, QR + 2 * EXTI, UB), F32), pltpu.VMEM((ACC_ROWS, 4 * UB), F32),
            pltpu.VMEM((2, NP // 128, HALF, 2, 128), BF16),
            pltpu.VMEM((128, 512), F32), pltpu.VMEM((128, 512), F32), pltpu.VMEM((32, 512), F32), pltpu.VMEM((32, 512), F32),
            pltpu.VMEM((NP, 512), BF16), pltpu.VMEM((NP, 512), BF16), pltpu.VMEM((4, 2 * HALF, 128), F32),
            pltpu.VMEM((ROWS, PR, 128), BF16), pltpu.VMEM((ROWS, PR, 128), BF16),
            pltpu.VMEM((2, 2 * QR, 512), F32), pltpu.VMEM((WAVES, QR, UB), BF16),
            pltpu.VMEM((WAVES, QE, UB), I32), pltpu.VMEM((WAVES, QE, UB), I32), pltpu.VMEM((QE, UB), I32),
            pltpu.VMEM((WAVES, QE, UB), I32), pltpu.VMEM((WAVES, QE, UB), I32), pltpu.VMEM((WAVES, QE, UB), F32),
            dma((2, NP // 128)), dma((3,)), dma((2, ROWS)), dma((2, ROWS)), dma((WAVES,)), dma((WAVES,)),
            dma((2, WAVES)), dma((2, WAVES)), dma((6,)), dma((6,)),
        ],
        compiler_params=pltpu.CompilerParams(collective_id=0, has_side_effects=True, vmem_limit_bytes=50 << 20),
    )(wave_scale, *[pltpu.with_memory_space_constraint(v, pltpu.HBM) for v in (x, trace_start, trace_length, column_slot)])


def solution(mesh):
    placed = (
        P("wave", "row", None, None),
        P("wave"),
        P(None, "row", "wave"),
        P(None, "row", "wave"),
        P("row", "wave"),
    )
    return jax.shard_map(
        per_device, mesh=mesh, in_specs=placed, out_specs=P("row", "wave"), check_vma=False
    )
```

```python
import jax
import jax.numpy as jnp
from jax import lax
from jax.experimental import pallas as pl
from jax.experimental.pallas import tpu as pltpu
from jax.sharding import PartitionSpec as P

F32, BF16, I32 = jnp.float32, jnp.bfloat16, jnp.int32
MESH = pl.DeviceIdType.MESH
NP = 4096
NQ = 1024
ROWS = 16
WAVES = 8
PR = NP // ROWS
QR = NQ // ROWS
UB = NQ // WAVES
EXT = 8
EXTI = 16
HALF = PR // 2
QE = QR + 2 * EXT
PAIRS = 36
ACC_ROWS = 8 * PAIRS + 40


def sincos_turns(turns):
    frac = turns - jnp.round(turns)
    quad = jnp.round(frac * 4.0)
    r = (frac - quad * 0.25) * 6.283185307179586
    r2 = r * r
    s = r * (1.0 + r2 * (-1.6666667e-1 + r2 * (8.3333310e-3 + r2 * (-1.9840874e-4 + r2 * 2.7525562e-6))))
    c = 1.0 + r2 * (-0.5 + r2 * (4.16666642e-2 + r2 * (-1.3888397e-3 + r2 * 2.4760495e-5)))
    odd = jnp.abs(quad) == 1.0
    cc = jnp.where(odd, s, c)
    ss = jnp.where(odd, c, s)
    cneg = (quad == 1.0) | (jnp.abs(quad) == 2.0)
    sneg = (quad == -1.0) | (jnp.abs(quad) == 2.0)
    return jnp.where(cneg, -cc, cc), jnp.where(sneg, -ss, ss)


def lane_sign(shape):
    return jnp.where(lax.broadcasted_iota(I32, shape, 1) < 64, 1.0, -1.0).astype(F32)


def lane_order(wave):
    n = lax.broadcasted_iota(I32, (UB, UB), 0)
    x = lax.broadcasted_iota(I32, (UB, UB), 1)
    return (n == jnp.where(wave >= WAVES // 2, UB - 1 - x, x)).astype(F32).astype(BF16)


def window(w, odd):
    return range((w + 4 * odd) // 8, (w + 4 * odd + 22) // 8 + 1)


def k1(scale_ref, x_ref, start_ref, length_ref, slot_ref,
       out_ref,
       light_ref, slots_ref, spread_ref, mask, lf, image,
       xv, lo_u, lo_v, hi_c, hi_s, tab0, tab1, acc, sbuf, rbuf, zacc, ibuf, start_v, length_v, slot_v, begin_v, count_v, gain_v,
       x_sem, own_sem, y_send, y_recv, i_send, i_recv, e_send, e_recv, t_send, t_recv):
    wave = lax.axis_index("wave")
    row = lax.axis_index("row")
    below = lax.rem(row + 1, ROWS)
    above = lax.rem(row + ROWS - 1, ROWS)
    tabs = (tab0, tab1)

    def fetch(h, c):
        return pltpu.make_async_copy(x_ref.at[pl.ds(HALF * h, HALF), c], xv.at[h, c], x_sem.at[h, c])

    for c in range(32):
        fetch(0, c).start()

    barrier = pltpu.get_barrier_semaphore()

    def greet_row(i, carry):
        pl.semaphore_signal(barrier, inc=1, device_id=(wave, lax.rem(row + i, ROWS)), device_id_type=MESH)
        return carry

    def greet_wave(i, carry):
        pl.semaphore_signal(barrier, inc=1, device_id=(lax.rem(wave + i, WAVES), row), device_id_type=MESH)
        pl.semaphore_signal(barrier, inc=1, device_id=(lax.rem(wave + i, WAVES), below), device_id_type=MESH)
        pl.semaphore_signal(barrier, inc=1, device_id=(lax.rem(wave + i, WAVES), above), device_id_type=MESH)
        return carry

    lax.fori_loop(1, ROWS, greet_row, 0)
    lax.fori_loop(1, WAVES, greet_wave, 0)

    mid = slice(EXT, EXT + QR)
    locals_ = [
        pltpu.make_async_copy(start_ref, start_v.at[:, mid, :], own_sem.at[0]),
        pltpu.make_async_copy(length_ref, length_v.at[:, mid, :], own_sem.at[1]),
        pltpu.make_async_copy(slot_ref, slot_v.at[mid, :], own_sem.at[2]),
    ]
    for copy in locals_:
        copy.start()

    first = lax.rem(row + row // 4, 2)
    s = scale_ref[0] * (1.0 / NP)

    def make_table(t):
        j = first if t == 0 else 1 - first
        low = lax.broadcasted_iota(I32, (128, 128), 1) < 64
        for v in range(2):
            n = lax.broadcasted_iota(I32, (1, 128), 1)
            k = 64 * (2 * (2 * v + n // 64) + j) + n % 64
            y = k.astype(F32) - 511.5
            b = lax.broadcasted_iota(I32, (128, 128), 0).astype(F32) - 63.5
            c, sn = sincos_turns(b * y * s)
            c = c * (1.0 / 64.0)
            sn = sn * (1.0 / 64.0)
            cr = pltpu.roll(c, 64, 1)
            sr = pltpu.roll(sn, 64, 1)
            one, two = slice(256 * v, 256 * v + 128), slice(256 * v + 128, 256 * v + 256)
            lo_u[:, one] = jnp.where(low, c, sr)
            lo_u[:, two] = jnp.where(low, cr, sn)
            lo_v[:, one] = jnp.where(low, -sn, cr)
            lo_v[:, two] = jnp.where(low, -sr, c)
            a = lax.broadcasted_iota(I32, (32, 128), 0).astype(F32) * 128.0 - 1984.0
            c, sn = sincos_turns(a * y * s)
            cr = pltpu.roll(c, 64, 1)
            sr = pltpu.roll(sn, 64, 1)
            hi_c[:, one] = jnp.where(low[0:32], c, cr)
            hi_c[:, two] = jnp.where(low[0:32], cr, c)
            hi_s[:, one] = jnp.where(low[0:32], sn, sr)
            hi_s[:, two] = jnp.where(low[0:32], sr, sn)

        def make(a, carry):
            rows = pl.ds(pl.multiple_of(a * 128, 128), 128)
            tabs[t][rows, :] = (lo_u[...] * hi_c[pl.ds(a, 1), :] + lo_v[...] * hi_s[pl.ds(a, 1), :]).astype(BF16)
            return carry

        lax.fori_loop(0, 32, make, 0)

    sgn = lane_sign((HALF, 128))

    def edge_copies():
        def cp(src, dst, i, dev):
            return pltpu.make_async_remote_copy(src_ref=src, dst_ref=dst, send_sem=t_send.at[i], recv_sem=t_recv.at[i],
                                                device_id=(wave, dev), device_id_type=MESH)
        last = slice(QR - EXT, QR)
        head = slice(0, EXT)
        tail = slice(EXT + QR, QR + 2 * EXT)
        return [
            cp(start_ref.at[:, last, :], start_v.at[:, head, :], 0, below),
            cp(length_ref.at[:, last, :], length_v.at[:, head, :], 1, below),
            cp(slot_ref.at[last, :], slot_v.at[head, :], 2, below),
            cp(start_ref.at[:, head, :], start_v.at[:, tail, :], 3, above),
            cp(length_ref.at[:, head, :], length_v.at[:, tail, :], 4, above),
            cp(slot_ref.at[head, :], slot_v.at[tail, :], 5, above),
        ]

    def part(h):
        return pl.ds(pl.multiple_of(HALF * h, HALF), HALF)

    def y_copy(dest, h):
        return pltpu.make_async_remote_copy(src_ref=sbuf.at[dest, part(h)], dst_ref=rbuf.at[row, part(h)], send_sem=y_send.at[h, dest],
                                            recv_sem=y_recv.at[h, row], device_id=(wave, dest), device_id_type=MESH)

    def y_local(h):
        return pltpu.make_async_copy(sbuf.at[row, part(h)], rbuf.at[row, part(h)], y_recv.at[h, row])

    def y_arrival(src, h):
        return pltpu.make_async_remote_copy(src_ref=sbuf.at[src, part(h)], dst_ref=rbuf.at[src, part(h)], send_sem=y_send.at[h, src],
                                            recv_sem=y_recv.at[h, src], device_id=(wave, src), device_id_type=MESH)

    for t in range(2):
        make_table(t)
        if t == 0:
            for c in range(32):
                fetch(1, c).start()
        j = first if t == 0 else 1 - first

        def block(h, carry):
            if t == 0:
                def arrived(c, carry):
                    fetch(h, c).wait()
                    return carry

                lax.fori_loop(0, 32, arrived, 0)
            field = jnp.concatenate([xv.at[h, c].reshape(2 * HALF, 128)[...] for c in range(32)], axis=1)
            y = jnp.dot(field, tabs[t][...], preferred_element_type=F32)
            for i in range(4):
                acc[i] = y[:, 128 * i:128 * i + 128]
            if t == 0:
                @pl.when(h == 0)
                def _():
                    pl.semaphore_wait(barrier, 36)

            def message(n, carry):
                i = lax.rem(n + 2 * lax.rem(row // 4, 2) + lax.rem(row, 4) // 2, 4)
                p = acc[i, pl.ds(0, HALF, stride=2), :]
                r = pltpu.roll(acc[i, pl.ds(1, HALF, stride=2), :], 64, 1)
                direct = 2 * i + j
                mirror = ROWS - 1 - direct
                sbuf[direct, part(h), :] = (r + sgn * p).astype(BF16)
                sbuf[mirror, part(h), :] = (p - sgn * r).astype(BF16)
                for dest in (direct, mirror):
                    @pl.when(dest != row)
                    def _():
                        y_copy(dest, h).start()

                    @pl.when(dest == row)
                    def _():
                        y_local(h).start()
                return carry

            lax.fori_loop(0, 4, message, 0)
            return carry

        lax.fori_loop(0, 2, block, 0)
        if t == 0:
            for copy in edge_copies():
                copy.start()

    zacc[...] = jnp.zeros_like(zacc)
    mine = lax.rem(jnp.where(row < ROWS // 2, row, ROWS - 1 - row), 2)

    def source(i):
        y = lax.rem(row // 4 + lax.rem(i, 8) // 2, 4)
        return 4 * y + 2 * lax.rem(i, 2) + lax.rem(mine + y + i // 8, 2)

    def absorb(t, carry):
        srcs = [source(2 * t + i) for i in range(2)]
        for src in srcs:
            for h in range(2):
                @pl.when(src == row)
                def _():
                    y_local(h).wait()

                @pl.when(src != row)
                def _():
                    y_arrival(src, h).wait_recv()

        for k in range(2):
            total = None
            for src in srcs:
                rows = pl.ds(pl.multiple_of(src * PR, PR), PR)
                z = lax.dot_general(rbuf[src], tabs[k][rows, :], (((0,), (0,)), ((), ())), preferred_element_type=F32)
                total = z if total is None else total + z
            zacc[k] += total
        return carry

    lax.fori_loop(0, ROWS // 2, absorb, 0)

    flip = row >= ROWS // 2
    last_rows = pl.ds(pl.multiple_of(jnp.where(flip, 0, QR - EXTI), EXTI), EXTI)
    first_rows = pl.ds(pl.multiple_of(jnp.where(flip, QR - EXTI, 0), EXTI), EXTI)
    main = pl.ds(EXTI, QR)
    headi = pl.ds(0, EXTI)
    taili = pl.ds(EXTI + QR, EXTI)

    def i_copy(dest):
        return pltpu.make_async_remote_copy(src_ref=ibuf.at[dest], dst_ref=light_ref.at[wave, main, :], send_sem=i_send.at[dest],
                                            recv_sem=i_recv.at[wave], device_id=(dest, row), device_id_type=MESH)

    def top_copy(dest):
        return pltpu.make_async_remote_copy(src_ref=ibuf.at[dest, last_rows, :], dst_ref=light_ref.at[wave, headi, :], send_sem=e_send.at[0, dest],
                                            recv_sem=e_recv.at[0, wave], device_id=(dest, below), device_id_type=MESH)

    def bot_copy(dest):
        return pltpu.make_async_remote_copy(src_ref=ibuf.at[dest, first_rows, :], dst_ref=light_ref.at[wave, taili, :], send_sem=e_send.at[1, dest],
                                            recv_sem=e_recv.at[1, wave], device_id=(dest, above), device_id_type=MESH)

    def own():
        return pltpu.make_async_copy(ibuf.at[wave], light_ref.at[wave, main, :], i_recv.at[wave])

    sgz = lane_sign((QR, 128))
    low = lax.broadcasted_iota(I32, (QR, 128), 1) < 64

    def intensities(m, carry):
        cols = pl.ds(pl.multiple_of(128 * m, 128), 128)
        direct, mirror = [], []
        for blk in range(2):
            k = jnp.where(first == blk, 0, 1)
            p = zacc[k, 0:QR, cols]
            r = pltpu.roll(zacc[k, QR:2 * QR, cols], 64, 1)
            z1 = r + sgz * p
            z2 = p - sgz * r
            z1 = z1 * z1
            z2 = z2 * z2
            direct.append(z1 + pltpu.roll(z1, 64, 1))
            mirror.append(z2 + pltpu.roll(z2, 64, 1))
        ibuf[m] = jnp.where(low, direct[0], direct[1]).astype(BF16)
        ibuf[WAVES - 1 - m] = jnp.where(low, mirror[0], mirror[1]).astype(BF16)
        for dest in (m, WAVES - 1 - m):
            @pl.when(dest != wave)
            def _():
                i_copy(dest).start()

            @pl.when(dest == wave)
            def _():
                own().start()
            top_copy(dest).start()
            bot_copy(dest).start()
        return carry

    lax.fori_loop(0, 4, intensities, 0)

    for copy in locals_:
        copy.wait()
    for copy in edge_copies():
        copy.wait()
    order = lane_order(wave)
    q = lax.broadcasted_iota(I32, (QE, UB), 0)
    base = 4 * (row * QR + q - EXT) - 8 - 4 * (q % 2)

    def prepare(w, carry):
        begin = jnp.clip(start_v[w] - base, -64, 64).astype(F32).astype(BF16)
        begin = jnp.dot(begin, order, preferred_element_type=F32)
        length = jnp.dot(length_v[w].astype(F32).astype(BF16), order, preferred_element_type=F32)
        begin_v[w] = begin.astype(I32)
        count_v[w] = length.astype(I32)
        gain_v[w] = 1.0 / length
        return carry

    lax.fori_loop(0, WAVES, prepare, 0)
    slots_ref[...] = jnp.dot(slot_v[...].astype(F32).astype(BF16), order, preferred_element_type=F32).astype(I32)
    n = lax.broadcasted_iota(I32, (4 * UB, 4 * UB), 0)
    x = lax.broadcasted_iota(I32, (4 * UB, 4 * UB), 1)
    lane = n % UB
    lane = jnp.where(wave >= WAVES // 2, UB - 1 - lane, lane)
    spread_ref[...] = (4 * lane + n // UB == x).astype(F32).astype(BF16)
    sub = lax.broadcasted_iota(I32, (8, UB), 0)

    def make_masks(j, carry):
        for odd in range(2):
            q = 2 * (j + 1) + odd
            for w in range(WAVES):
                f = jnp.broadcast_to(begin_v[w, pl.ds(q, 1), :], (8, UB))
                e = jnp.broadcast_to(count_v[w, pl.ds(q, 1), :], (8, UB)).astype(jnp.uint32)
                g = jnp.broadcast_to(gain_v[w, pl.ds(q, 1), :], (8, UB))
                for k, i in enumerate(window(w, odd)):
                    mask[w, j, odd, 8 * k:8 * k + 8, :] = jnp.where((sub + 8 * i - f).astype(jnp.uint32) < e, g, 0.0)
        return carry

    lax.fori_loop(0, PAIRS, make_masks, 0)
    image[...] = jnp.zeros_like(image)

    def drain(t, carry):
        for h in range(2):
            y_copy(lax.rem(row + t, ROWS), h).wait_send()
        return carry

    lax.fori_loop(1, ROWS, drain, 0)

    def i_arrival(src):
        return pltpu.make_async_remote_copy(src_ref=ibuf.at[src], dst_ref=light_ref.at[src, main, :], send_sem=i_send.at[src],
                                            recv_sem=i_recv.at[src], device_id=(src, row), device_id_type=MESH)

    def top_arrival(src):
        return pltpu.make_async_remote_copy(src_ref=ibuf.at[src, last_rows, :], dst_ref=light_ref.at[src, headi, :], send_sem=e_send.at[0, src],
                                            recv_sem=e_recv.at[0, src], device_id=(src, below), device_id_type=MESH)

    def bot_arrival(src):
        return pltpu.make_async_remote_copy(src_ref=ibuf.at[src, first_rows, :], dst_ref=light_ref.at[src, taili, :], send_sem=e_send.at[1, src],
                                            recv_sem=e_recv.at[1, src], device_id=(src, above), device_id_type=MESH)

    def finish(t, carry):
        src = lax.rem(wave + t, WAVES)

        @pl.when(t != 0)
        def _():
            i_arrival(src).wait()

        @pl.when(t == 0)
        def _():
            own().wait()
        return carry

    def finish_edges(src, carry):
        top_arrival(src).wait()
        bot_arrival(src).wait()
        return carry

    lax.fori_loop(0, WAVES, finish, 0)
    flip_above = above >= ROWS // 2
    flip_below = below >= ROWS // 2
    def held(q):
        n = q - EXT
        top = jnp.where(flip_above, 7 - q, 8 + q)
        mid_at = EXTI + jnp.where(flip, QR - 1 - n, n)
        n = q - EXT - QR
        bot = EXTI + QR + jnp.where(flip_below, EXTI - 1 - n, n)
        return jnp.where(q < EXT, top, jnp.where(q < EXT + QR, mid_at, bot))

    def deposit(j, light):
        light = [list(groups) for groups in light]
        for odd in range(2):
            q = 2 * (j + 1) + odd
            at = held(q)
            strip = [None] * 5
            for w in range(WAVES):
                v = jnp.broadcast_to(lf[w, pl.ds(at, 1), :], (8, UB))
                for k, i in enumerate(window(w, odd)):
                    add = mask[w, j, odd, 8 * k:8 * k + 8, :] * v
                    strip[i] = add if strip[i] is None else strip[i] + add
            c = jnp.broadcast_to(slots_ref[pl.ds(q, 1), :], (8, UB))
            for k in range(4):
                hot = c == k
                for i in range(5):
                    if strip[i] is not None:
                        add = jnp.where(hot, strip[i], 0.0)
                        light[k][i] = add if light[k][i] is None else light[k][i] + add
        return light

    def group(j):
        return pl.ds(pl.multiple_of(8 * j, 8), 8)

    def pair(j, carry):
        light = deposit(j, [list(carry[4 * k:4 * k + 4]) + [None] for k in range(4)])
        for k in range(4):
            image[group(j), UB * k:UB * k + UB] = light[k][0]
        return tuple(light[k][i] for k in range(4) for i in range(1, 5))

    def edge_pair(n, carry):
        j = jnp.where(n < 3, n, PAIRS - 1)
        light = deposit(j, [[None] * 5 for _ in range(4)])
        for k in range(4):
            for i in range(5):
                image[group(j + i), UB * k:UB * k + UB] += light[k][i]
        return carry

    lf[:, EXTI:EXTI + QR, :] = light_ref[:, EXTI:EXTI + QR, :].astype(F32)
    zero = jnp.zeros((8, UB), F32)
    carry = lax.fori_loop(3, PAIRS - 1, pair, (zero,) * 16, unroll=2)
    for k in range(4):
        for i in range(4):
            image[8 * (PAIRS - 1 + i):8 * (PAIRS + i), UB * k:UB * k + UB] = carry[4 * k + i]
    lax.fori_loop(0, WAVES, finish_edges, 0)
    lf[:, 0:EXTI, :] = light_ref[:, 0:EXTI, :].astype(F32)
    lf[:, EXTI + QR:, :] = light_ref[:, EXTI + QR:, :].astype(F32)
    lax.fori_loop(0, 4, edge_pair, 0)
    whole = image[32:32 + 4 * QR, :]
    hi = whole.astype(BF16)
    lo = (whole - hi.astype(F32)).astype(BF16)
    spread = spread_ref[...]
    out_ref[...] = jnp.dot(hi, spread, preferred_element_type=F32) + jnp.dot(lo, spread, preferred_element_type=F32)


def per_device(lyot_field, wave_scale, trace_start, trace_length, column_slot):
    x = lyot_field.reshape(PR, 2, NP // 128, 128).transpose(0, 2, 1, 3)
    vm = pl.BlockSpec(memory_space=pltpu.VMEM)
    hbm = pl.BlockSpec(memory_space=pltpu.HBM)
    dma = pltpu.SemaphoreType.DMA
    return pl.pallas_call(
        k1,
        out_shape=jax.ShapeDtypeStruct((4 * QR, 4 * UB), F32),
        in_specs=[pl.BlockSpec(memory_space=pltpu.SMEM), hbm, hbm, hbm, hbm],
        out_specs=vm,
        scratch_shapes=[
            pltpu.VMEM((WAVES, QR + 2 * EXTI, UB), BF16), pltpu.VMEM((QE, UB), I32), pltpu.VMEM((4 * UB, 4 * UB), BF16),
            pltpu.VMEM((WAVES, PAIRS, 2, 32, UB), F32), pltpu.VMEM((WAVES, QR + 2 * EXTI, UB), F32), pltpu.VMEM((ACC_ROWS, 4 * UB), F32),
            pltpu.VMEM((2, NP // 128, HALF, 2, 128), BF16),
            pltpu.VMEM((128, 512), F32), pltpu.VMEM((128, 512), F32), pltpu.VMEM((32, 512), F32), pltpu.VMEM((32, 512), F32),
            pltpu.VMEM((NP, 512), BF16), pltpu.VMEM((NP, 512), BF16), pltpu.VMEM((4, 2 * HALF, 128), F32),
            pltpu.VMEM((ROWS, PR, 128), BF16), pltpu.VMEM((ROWS, PR, 128), BF16),
            pltpu.VMEM((2, 2 * QR, 512), F32), pltpu.VMEM((WAVES, QR, UB), BF16),
            pltpu.VMEM((WAVES, QE, UB), I32), pltpu.VMEM((WAVES, QE, UB), I32), pltpu.VMEM((QE, UB), I32),
            pltpu.VMEM((WAVES, QE, UB), I32), pltpu.VMEM((WAVES, QE, UB), I32), pltpu.VMEM((WAVES, QE, UB), F32),
            dma((2, NP // 128)), dma((3,)), dma((2, ROWS)), dma((2, ROWS)), dma((WAVES,)), dma((WAVES,)),
            dma((2, WAVES)), dma((2, WAVES)), dma((6,)), dma((6,)),
        ],
        compiler_params=pltpu.CompilerParams(collective_id=0, has_side_effects=True, vmem_limit_bytes=50 << 20),
    )(wave_scale, *[pltpu.with_memory_space_constraint(v, pltpu.HBM) for v in (x, trace_start, trace_length, column_slot)])


def solution(mesh):
    placed = (
        P("wave", "row", None, None),
        P("wave"),
        P(None, "row", "wave"),
        P(None, "row", "wave"),
        P("row", "wave"),
    )
    return jax.shard_map(
        per_device, mesh=mesh, in_specs=placed, out_specs=P("row", "wave"), check_vma=False
    )
```

```python
import jax
import jax.numpy as jnp
from jax import lax
from jax.experimental import pallas as pl
from jax.experimental.pallas import tpu as pltpu
from jax.sharding import PartitionSpec as P

F32, BF16, I32 = jnp.float32, jnp.bfloat16, jnp.int32
MESH = pl.DeviceIdType.MESH
NP = 4096
NQ = 1024
ROWS = 16
WAVES = 8
PR = NP // ROWS
QR = NQ // ROWS
UB = NQ // WAVES
EXT = 8
EXTI = 16
HALF = PR // 2
QE = QR + 2 * EXT
PAIRS = 36
ACC_ROWS = 8 * PAIRS + 40


def sincos_turns(turns):
    frac = turns - jnp.round(turns)
    quad = jnp.round(frac * 4.0)
    r = (frac - quad * 0.25) * 6.283185307179586
    r2 = r * r
    s = r * (1.0 + r2 * (-1.6666667e-1 + r2 * (8.3333310e-3 + r2 * (-1.9840874e-4 + r2 * 2.7525562e-6))))
    c = 1.0 + r2 * (-0.5 + r2 * (4.16666642e-2 + r2 * (-1.3888397e-3 + r2 * 2.4760495e-5)))
    odd = jnp.abs(quad) == 1.0
    cc = jnp.where(odd, s, c)
    ss = jnp.where(odd, c, s)
    cneg = (quad == 1.0) | (jnp.abs(quad) == 2.0)
    sneg = (quad == -1.0) | (jnp.abs(quad) == 2.0)
    return jnp.where(cneg, -cc, cc), jnp.where(sneg, -ss, ss)


def lane_sign(shape):
    return jnp.where(lax.broadcasted_iota(I32, shape, 1) < 64, 1.0, -1.0).astype(F32)


def lane_order(wave):
    n = lax.broadcasted_iota(I32, (UB, UB), 0)
    x = lax.broadcasted_iota(I32, (UB, UB), 1)
    return (n == jnp.where(wave >= WAVES // 2, UB - 1 - x, x)).astype(F32).astype(BF16)


def window(w, odd):
    return range((w + 4 * odd) // 8, (w + 4 * odd + 22) // 8 + 1)


def k1(scale_ref, x_ref, start_ref, length_ref, slot_ref,
       out_ref,
       light_ref, slots_ref, spread_ref, mask, lf, image,
       xv, lo_u, lo_v, hi_c, hi_s, tab0, tab1, acc, sbuf, rbuf, zacc, ibuf, start_v, length_v, slot_v, begin_v, count_v, gain_v,
       x_sem, own_sem, y_send, y_recv, i_send, i_recv, e_send, e_recv, t_send, t_recv):
    wave = lax.axis_index("wave")
    row = lax.axis_index("row")
    below = lax.rem(row + 1, ROWS)
    above = lax.rem(row + ROWS - 1, ROWS)
    tabs = (tab0, tab1)

    def fetch(h, c):
        return pltpu.make_async_copy(x_ref.at[pl.ds(HALF * h, HALF), c], xv.at[h, c], x_sem.at[h, c])

    for c in range(32):
        fetch(0, c).start()

    barrier = pltpu.get_barrier_semaphore()

    def greet_row(i, carry):
        pl.semaphore_signal(barrier, inc=1, device_id=(wave, lax.rem(row + i, ROWS)), device_id_type=MESH)
        return carry

    def greet_wave(i, carry):
        pl.semaphore_signal(barrier, inc=1, device_id=(lax.rem(wave + i, WAVES), row), device_id_type=MESH)
        pl.semaphore_signal(barrier, inc=1, device_id=(lax.rem(wave + i, WAVES), below), device_id_type=MESH)
        pl.semaphore_signal(barrier, inc=1, device_id=(lax.rem(wave + i, WAVES), above), device_id_type=MESH)
        return carry

    lax.fori_loop(1, ROWS, greet_row, 0)
    lax.fori_loop(1, WAVES, greet_wave, 0)

    mid = slice(EXT, EXT + QR)
    locals_ = [
        pltpu.make_async_copy(start_ref, start_v.at[:, mid, :], own_sem.at[0]),
        pltpu.make_async_copy(length_ref, length_v.at[:, mid, :], own_sem.at[1]),
        pltpu.make_async_copy(slot_ref, slot_v.at[mid, :], own_sem.at[2]),
    ]
    for copy in locals_:
        copy.start()

    first = lax.rem(row + row // 4, 2)
    s = scale_ref[0] * (1.0 / NP)

    def make_table(t):
        j = first if t == 0 else 1 - first
        low = lax.broadcasted_iota(I32, (128, 128), 1) < 64
        for v in range(2):
            n = lax.broadcasted_iota(I32, (1, 128), 1)
            k = 64 * (2 * (2 * v + n // 64) + j) + n % 64
            y = k.astype(F32) - 511.5
            b = lax.broadcasted_iota(I32, (128, 128), 0).astype(F32) - 63.5
            c, sn = sincos_turns(b * y * s)
            c = c * (1.0 / 64.0)
            sn = sn * (1.0 / 64.0)
            cr = pltpu.roll(c, 64, 1)
            sr = pltpu.roll(sn, 64, 1)
            one, two = slice(256 * v, 256 * v + 128), slice(256 * v + 128, 256 * v + 256)
            lo_u[:, one] = jnp.where(low, c, sr)
            lo_u[:, two] = jnp.where(low, cr, sn)
            lo_v[:, one] = jnp.where(low, -sn, cr)
            lo_v[:, two] = jnp.where(low, -sr, c)
            a = lax.broadcasted_iota(I32, (32, 128), 0).astype(F32) * 128.0 - 1984.0
            c, sn = sincos_turns(a * y * s)
            cr = pltpu.roll(c, 64, 1)
            sr = pltpu.roll(sn, 64, 1)
            hi_c[:, one] = jnp.where(low[0:32], c, cr)
            hi_c[:, two] = jnp.where(low[0:32], cr, c)
            hi_s[:, one] = jnp.where(low[0:32], sn, sr)
            hi_s[:, two] = jnp.where(low[0:32], sr, sn)

        def make(a, carry):
            rows = pl.ds(pl.multiple_of(a * 128, 128), 128)
            tabs[t][rows, :] = (lo_u[...] * hi_c[pl.ds(a, 1), :] + lo_v[...] * hi_s[pl.ds(a, 1), :]).astype(BF16)
            return carry

        lax.fori_loop(0, 32, make, 0)

    sgn = lane_sign((HALF, 128))

    def edge_copies():
        def cp(src, dst, i, dev):
            return pltpu.make_async_remote_copy(src_ref=src, dst_ref=dst, send_sem=t_send.at[i], recv_sem=t_recv.at[i],
                                                device_id=(wave, dev), device_id_type=MESH)
        last = slice(QR - EXT, QR)
        head = slice(0, EXT)
        tail = slice(EXT + QR, QR + 2 * EXT)
        return [
            cp(start_ref.at[:, last, :], start_v.at[:, head, :], 0, below),
            cp(length_ref.at[:, last, :], length_v.at[:, head, :], 1, below),
            cp(slot_ref.at[last, :], slot_v.at[head, :], 2, below),
            cp(start_ref.at[:, head, :], start_v.at[:, tail, :], 3, above),
            cp(length_ref.at[:, head, :], length_v.at[:, tail, :], 4, above),
            cp(slot_ref.at[head, :], slot_v.at[tail, :], 5, above),
        ]

    def part(h):
        return pl.ds(pl.multiple_of(HALF * h, HALF), HALF)

    def y_copy(dest, h):
        return pltpu.make_async_remote_copy(src_ref=sbuf.at[dest, part(h)], dst_ref=rbuf.at[row, part(h)], send_sem=y_send.at[h, dest],
                                            recv_sem=y_recv.at[h, row], device_id=(wave, dest), device_id_type=MESH)

    def y_local(h):
        return pltpu.make_async_copy(sbuf.at[row, part(h)], rbuf.at[row, part(h)], y_recv.at[h, row])

    def y_arrival(src, h):
        return pltpu.make_async_remote_copy(src_ref=sbuf.at[src, part(h)], dst_ref=rbuf.at[src, part(h)], send_sem=y_send.at[h, src],
                                            recv_sem=y_recv.at[h, src], device_id=(wave, src), device_id_type=MESH)

    for t in range(2):
        make_table(t)
        if t == 0:
            for c in range(32):
                fetch(1, c).start()
        j = first if t == 0 else 1 - first

        def block(h, carry):
            if t == 0:
                def arrived(c, carry):
                    fetch(h, c).wait()
                    return carry

                lax.fori_loop(0, 32, arrived, 0)
            field = jnp.concatenate([xv.at[h, c].reshape(2 * HALF, 128)[...] for c in range(32)], axis=1)
            y = jnp.dot(field, tabs[t][...], preferred_element_type=F32)
            for i in range(4):
                acc[i] = y[:, 128 * i:128 * i + 128]
            if t == 0:
                @pl.when(h == 0)
                def _():
                    pl.semaphore_wait(barrier, 36)

            def message(n, carry):
                i = lax.rem(n + 2 * lax.rem(row // 4, 2) + lax.rem(row, 4) // 2, 4)
                p = acc[i, pl.ds(0, HALF, stride=2), :]
                r = pltpu.roll(acc[i, pl.ds(1, HALF, stride=2), :], 64, 1)
                direct = 2 * i + j
                mirror = ROWS - 1 - direct
                sbuf[direct, part(h), :] = (r + sgn * p).astype(BF16)
                sbuf[mirror, part(h), :] = (p - sgn * r).astype(BF16)
                for dest in (direct, mirror):
                    @pl.when(dest != row)
                    def _():
                        y_copy(dest, h).start()

                    @pl.when(dest == row)
                    def _():
                        y_local(h).start()
                return carry

            lax.fori_loop(0, 4, message, 0)
            return carry

        lax.fori_loop(0, 2, block, 0)
        if t == 0:
            for copy in edge_copies():
                copy.start()

    zacc[...] = jnp.zeros_like(zacc)
    mine = lax.rem(jnp.where(row < ROWS // 2, row, ROWS - 1 - row), 2)

    def source(i):
        y = lax.rem(row // 4 + lax.rem(i, 8) // 2, 4)
        return 4 * y + 2 * lax.rem(i, 2) + lax.rem(mine + y + i // 8, 2)

    def absorb(t, carry):
        srcs = [source(2 * t + i) for i in range(2)]
        for src in srcs:
            for h in range(2):
                @pl.when(src == row)
                def _():
                    y_local(h).wait()

                @pl.when(src != row)
                def _():
                    y_arrival(src, h).wait_recv()

        for k in range(2):
            total = None
            for src in srcs:
                rows = pl.ds(pl.multiple_of(src * PR, PR), PR)
                z = lax.dot_general(rbuf[src], tabs[k][rows, :], (((0,), (0,)), ((), ())), preferred_element_type=F32)
                total = z if total is None else total + z
            zacc[k] += total
        return carry

    lax.fori_loop(0, ROWS // 2, absorb, 0)

    flip = row >= ROWS // 2
    last_rows = pl.ds(pl.multiple_of(jnp.where(flip, 0, QR - EXTI), EXTI), EXTI)
    first_rows = pl.ds(pl.multiple_of(jnp.where(flip, QR - EXTI, 0), EXTI), EXTI)
    main = pl.ds(EXTI, QR)
    headi = pl.ds(0, EXTI)
    taili = pl.ds(EXTI + QR, EXTI)

    def i_copy(dest):
        return pltpu.make_async_remote_copy(src_ref=ibuf.at[dest], dst_ref=light_ref.at[wave, main, :], send_sem=i_send.at[dest],
                                            recv_sem=i_recv.at[wave], device_id=(dest, row), device_id_type=MESH)

    def top_copy(dest):
        return pltpu.make_async_remote_copy(src_ref=ibuf.at[dest, last_rows, :], dst_ref=light_ref.at[wave, headi, :], send_sem=e_send.at[0, dest],
                                            recv_sem=e_recv.at[0, wave], device_id=(dest, below), device_id_type=MESH)

    def bot_copy(dest):
        return pltpu.make_async_remote_copy(src_ref=ibuf.at[dest, first_rows, :], dst_ref=light_ref.at[wave, taili, :], send_sem=e_send.at[1, dest],
                                            recv_sem=e_recv.at[1, wave], device_id=(dest, above), device_id_type=MESH)

    def own():
        return pltpu.make_async_copy(ibuf.at[wave], light_ref.at[wave, main, :], i_recv.at[wave])

    sgz = lane_sign((QR, 128))
    low = lax.broadcasted_iota(I32, (QR, 128), 1) < 64

    def intensities(m, carry):
        cols = pl.ds(pl.multiple_of(128 * m, 128), 128)
        direct, mirror = [], []
        for blk in range(2):
            k = jnp.where(first == blk, 0, 1)
            p = zacc[k, 0:QR, cols]
            r = pltpu.roll(zacc[k, QR:2 * QR, cols], 64, 1)
            z1 = r + sgz * p
            z2 = p - sgz * r
            z1 = z1 * z1
            z2 = z2 * z2
            direct.append(z1 + pltpu.roll(z1, 64, 1))
            mirror.append(z2 + pltpu.roll(z2, 64, 1))
        ibuf[m] = jnp.where(low, direct[0], direct[1]).astype(BF16)
        ibuf[WAVES - 1 - m] = jnp.where(low, mirror[0], mirror[1]).astype(BF16)
        for dest in (m, WAVES - 1 - m):
            @pl.when(dest != wave)
            def _():
                i_copy(dest).start()

            @pl.when(dest == wave)
            def _():
                own().start()
            top_copy(dest).start()
            bot_copy(dest).start()
        return carry

    lax.fori_loop(0, 4, intensities, 0)

    for copy in locals_:
        copy.wait()
    for copy in edge_copies():
        copy.wait()
    order = lane_order(wave)
    q = lax.broadcasted_iota(I32, (QE, UB), 0)
    base = 4 * (row * QR + q - EXT) - 8 - 4 * (q % 2)

    def prepare(w, carry):
        begin = jnp.clip(start_v[w] - base, -64, 64).astype(F32).astype(BF16)
        begin = jnp.dot(begin, order, preferred_element_type=F32)
        length = jnp.dot(length_v[w].astype(F32).astype(BF16), order, preferred_element_type=F32)
        begin_v[w] = begin.astype(I32)
        count_v[w] = length.astype(I32)
        gain_v[w] = 1.0 / length
        return carry

    lax.fori_loop(0, WAVES, prepare, 0)
    slots_ref[...] = jnp.dot(slot_v[...].astype(F32).astype(BF16), order, preferred_element_type=F32).astype(I32)
    n = lax.broadcasted_iota(I32, (4 * UB, 4 * UB), 0)
    x = lax.broadcasted_iota(I32, (4 * UB, 4 * UB), 1)
    lane = n % UB
    lane = jnp.where(wave >= WAVES // 2, UB - 1 - lane, lane)
    spread_ref[...] = (4 * lane + n // UB == x).astype(F32).astype(BF16)
    sub = lax.broadcasted_iota(I32, (8, UB), 0)

    def make_masks(j, carry):
        for odd in range(2):
            q = 2 * (j + 1) + odd
            for w in range(WAVES):
                f = jnp.broadcast_to(begin_v[w, pl.ds(q, 1), :], (8, UB))
                e = jnp.broadcast_to(count_v[w, pl.ds(q, 1), :], (8, UB)).astype(jnp.uint32)
                g = jnp.broadcast_to(gain_v[w, pl.ds(q, 1), :], (8, UB))
                for k, i in enumerate(window(w, odd)):
                    mask[w, j, odd, 8 * k:8 * k + 8, :] = jnp.where((sub + 8 * i - f).astype(jnp.uint32) < e, g, 0.0)
        return carry

    lax.fori_loop(0, PAIRS, make_masks, 0)
    image[...] = jnp.zeros_like(image)

    def drain(t, carry):
        for h in range(2):
            y_copy(lax.rem(row + t, ROWS), h).wait_send()
        return carry

    lax.fori_loop(1, ROWS, drain, 0)

    def i_arrival(src):
        return pltpu.make_async_remote_copy(src_ref=ibuf.at[src], dst_ref=light_ref.at[src, main, :], send_sem=i_send.at[src],
                                            recv_sem=i_recv.at[src], device_id=(src, row), device_id_type=MESH)

    def top_arrival(src):
        return pltpu.make_async_remote_copy(src_ref=ibuf.at[src, last_rows, :], dst_ref=light_ref.at[src, headi, :], send_sem=e_send.at[0, src],
                                            recv_sem=e_recv.at[0, src], device_id=(src, below), device_id_type=MESH)

    def bot_arrival(src):
        return pltpu.make_async_remote_copy(src_ref=ibuf.at[src, first_rows, :], dst_ref=light_ref.at[src, taili, :], send_sem=e_send.at[1, src],
                                            recv_sem=e_recv.at[1, src], device_id=(src, above), device_id_type=MESH)

    def finish(t, carry):
        src = lax.rem(wave + t, WAVES)

        @pl.when(t != 0)
        def _():
            i_arrival(src).wait()

        @pl.when(t == 0)
        def _():
            own().wait()
        return carry

    def finish_edges(src, carry):
        top_arrival(src).wait()
        bot_arrival(src).wait()
        return carry

    lax.fori_loop(0, WAVES, finish, 0)
    flip_above = above >= ROWS // 2
    flip_below = below >= ROWS // 2
    def held(q):
        n = q - EXT
        top = jnp.where(flip_above, 7 - q, 8 + q)
        mid_at = EXTI + jnp.where(flip, QR - 1 - n, n)
        n = q - EXT - QR
        bot = EXTI + QR + jnp.where(flip_below, EXTI - 1 - n, n)
        return jnp.where(q < EXT, top, jnp.where(q < EXT + QR, mid_at, bot))

    def deposit(j, light):
        light = [list(groups) for groups in light]
        for odd in range(2):
            q = 2 * (j + 1) + odd
            at = held(q)
            strip = [None] * 5
            for w in range(WAVES):
                v = jnp.broadcast_to(lf[w, pl.ds(at, 1), :], (8, UB))
                for k, i in enumerate(window(w, odd)):
                    add = mask[w, j, odd, 8 * k:8 * k + 8, :] * v
                    strip[i] = add if strip[i] is None else strip[i] + add
            c = jnp.broadcast_to(slots_ref[pl.ds(q, 1), :], (8, UB))
            for k in range(4):
                hot = c == k
                for i in range(5):
                    if strip[i] is not None:
                        add = jnp.where(hot, strip[i], 0.0)
                        light[k][i] = add if light[k][i] is None else light[k][i] + add
        return light

    def group(j):
        return pl.ds(pl.multiple_of(8 * j, 8), 8)

    def pair(j, carry):
        light = deposit(j, [list(carry[4 * k:4 * k + 4]) + [None] for k in range(4)])
        for k in range(4):
            image[group(j), UB * k:UB * k + UB] = light[k][0]
        return tuple(light[k][i] for k in range(4) for i in range(1, 5))

    def edge_pair(n, carry):
        j = jnp.where(n < 3, n, PAIRS - 1)
        light = deposit(j, [[None] * 5 for _ in range(4)])
        for k in range(4):
            for i in range(5):
                image[group(j + i), UB * k:UB * k + UB] += light[k][i]
        return carry

    lf[:, EXTI:EXTI + QR, :] = light_ref[:, EXTI:EXTI + QR, :].astype(F32)
    zero = jnp.zeros((8, UB), F32)
    carry = lax.fori_loop(3, PAIRS - 1, pair, (zero,) * 16, unroll=4)
    for k in range(4):
        for i in range(4):
            image[8 * (PAIRS - 1 + i):8 * (PAIRS + i), UB * k:UB * k + UB] = carry[4 * k + i]
    lax.fori_loop(0, WAVES, finish_edges, 0)
    lf[:, 0:EXTI, :] = light_ref[:, 0:EXTI, :].astype(F32)
    lf[:, EXTI + QR:, :] = light_ref[:, EXTI + QR:, :].astype(F32)
    lax.fori_loop(0, 4, edge_pair, 0)
    whole = image[32:32 + 4 * QR, :]
    hi = whole.astype(BF16)
    lo = (whole - hi.astype(F32)).astype(BF16)
    spread = spread_ref[...]
    out_ref[...] = jnp.dot(hi, spread, preferred_element_type=F32) + jnp.dot(lo, spread, preferred_element_type=F32)


def per_device(lyot_field, wave_scale, trace_start, trace_length, column_slot):
    x = lyot_field.reshape(PR, 2, NP // 128, 128).transpose(0, 2, 1, 3)
    vm = pl.BlockSpec(memory_space=pltpu.VMEM)
    hbm = pl.BlockSpec(memory_space=pltpu.HBM)
    dma = pltpu.SemaphoreType.DMA
    return pl.pallas_call(
        k1,
        out_shape=jax.ShapeDtypeStruct((4 * QR, 4 * UB), F32),
        in_specs=[pl.BlockSpec(memory_space=pltpu.SMEM), hbm, hbm, hbm, hbm],
        out_specs=vm,
        scratch_shapes=[
            pltpu.VMEM((WAVES, QR + 2 * EXTI, UB), BF16), pltpu.VMEM((QE, UB), I32), pltpu.VMEM((4 * UB, 4 * UB), BF16),
            pltpu.VMEM((WAVES, PAIRS, 2, 32, UB), F32), pltpu.VMEM((WAVES, QR + 2 * EXTI, UB), F32), pltpu.VMEM((ACC_ROWS, 4 * UB), F32),
            pltpu.VMEM((2, NP // 128, HALF, 2, 128), BF16),
            pltpu.VMEM((128, 512), F32), pltpu.VMEM((128, 512), F32), pltpu.VMEM((32, 512), F32), pltpu.VMEM((32, 512), F32),
            pltpu.VMEM((NP, 512), BF16), pltpu.VMEM((NP, 512), BF16), pltpu.VMEM((4, 2 * HALF, 128), F32),
            pltpu.VMEM((ROWS, PR, 128), BF16), pltpu.VMEM((ROWS, PR, 128), BF16),
            pltpu.VMEM((2, 2 * QR, 512), F32), pltpu.VMEM((WAVES, QR, UB), BF16),
            pltpu.VMEM((WAVES, QE, UB), I32), pltpu.VMEM((WAVES, QE, UB), I32), pltpu.VMEM((QE, UB), I32),
            pltpu.VMEM((WAVES, QE, UB), I32), pltpu.VMEM((WAVES, QE, UB), I32), pltpu.VMEM((WAVES, QE, UB), F32),
            dma((2, NP // 128)), dma((3,)), dma((2, ROWS)), dma((2, ROWS)), dma((WAVES,)), dma((WAVES,)),
            dma((2, WAVES)), dma((2, WAVES)), dma((6,)), dma((6,)),
        ],
        compiler_params=pltpu.CompilerParams(collective_id=0, has_side_effects=True, vmem_limit_bytes=50 << 20),
    )(wave_scale, *[pltpu.with_memory_space_constraint(v, pltpu.HBM) for v in (x, trace_start, trace_length, column_slot)])


def solution(mesh):
    placed = (
        P("wave", "row", None, None),
        P("wave"),
        P(None, "row", "wave"),
        P(None, "row", "wave"),
        P("row", "wave"),
    )
    return jax.shard_map(
        per_device, mesh=mesh, in_specs=placed, out_specs=P("row", "wave"), check_vma=False
    )
```
